128 devices in a mesh: coil: 8 (over x, z_lo), slab: 16 (over y, z_hi, core).
Axes of the slice: x: 4, y: 4, z: 4 (z_hi: 2, z_lo: 2; z = z_hi * 2 + z_lo), core: 2. Of those that a mesh axis runs over, the one named last changes fastest.
Arguments:
- coil_maps: float32 [8, 2, 16, 256, 128], P('coil', None, 'slab'), may hold values from -1.5 to 1.5
- kspace: float32 [8, 2, 16, 256, 128], P('coil', None, 'slab'), may hold values from -6 to 6
- sample_mask: int32 [256, 128], replicated, may hold values 0 or 1
- iterate: float32 [2, 16, 256, 128], P(None, 'slab', 'coil'), may hold values from -6 to 6
- probe_bits: int32 [2, 16, 256, 128], P(None, 'slab', 'coil'), may hold values from 0 to 1
- loss_gradient: float32 [2, 16, 256, 128], P(None, 'slab', 'coil'), may hold values from -6 to 6
- adjoint: float32 [2, 16, 256, 128], P(None, 'slab', 'coil'), may hold values from -6 to 6
- kernel_first: bfloat16 [24, 2, 3, 3, 3], replicated, may hold values from -0.875 to 0.875
- kernel_second: bfloat16 [24, 24, 3, 3, 3], replicated, may hold values from -0.25 to 0.25
- kernel_last: bfloat16 [2, 24, 3, 3, 3], replicated, may hold values from -0.25 to 0.25
Outputs:
- new_iterate: float32 [2, 16, 256, 128], P(None, 'slab', 'coil')
- probe_pullback: float32 [2, 16, 256, 128], P(None, 'slab', 'coil')
- adjoint_next: float32 [2, 16, 256, 128], P(None, 'slab', 'coil')
The draws below stay inside these ranges and needn't reach their ends.
Inputs may be any that keep to these rules, and one draw needn't show every extreme that they name: `sample_mask`: 1 marks a sampled phase-encode line. `probe_bits`: the probe's sign is 2 p - 1.
All inputs are finite; a program needn't handle non-finite values.
Results may differ from the reference program's by a relative error of at most 0.0055.
Values may be sent and summed in bfloat16 or wider, within the bound.
No kernel may reach another device: no remote copies, remote signals or barrier semaphores. Data moves between devices by JAX's collectives and lax.ppermute only.
A program may use at most 128 MiB of HBM per device.

```python
import jax
import jax.numpy as jnp
from jax import lax

NC = 8
NY = 256
NZ = 128
CH = 24
NX = 16


def with_ends(entries, own_key, least, largest):
    shape = entries.shape
    place = [jax.random.randint(jax.random.fold_in(own_key, axis), (), 0, shape[axis]) for axis in range(len(shape))]
    entries = entries.at[tuple(place)].set(least)
    longest = shape.index(max(shape))
    place[longest] = (place[longest] + 1) % shape[longest]
    return entries.at[tuple(place)].set(largest)


def shard_levels(key, shape, pieces, low, high):
    factor_of = 1.0
    for axis_at, parts in pieces:
        heights = jax.random.uniform(jax.random.fold_in(jax.random.fold_in(key, 6), axis_at), (parts,), jnp.float32, low / len(pieces), high / len(pieces))
        factor_of = factor_of * jnp.repeat(jnp.exp(heights), shape[axis_at] // parts).reshape((-1,) + (1,) * (len(shape) - 1 - axis_at))
    return factor_of


def normal_values(stream_key, dims, deviation, bound, pieces=(), kind=jnp.bfloat16):
    values = deviation * jax.random.normal(stream_key, dims, jnp.float32)
    if pieces:
        values = values * shard_levels(stream_key, dims, pieces, -0.22, 0.18)
    return jnp.clip(values, -bound, bound).astype(kind)


def setup_inputs(seed: int = 0) -> dict:
    arg_keys = jax.random.split(jax.random.key(seed), 11)
    coil_maps = normal_values(arg_keys[0], (NC, 2, NX, NY, NZ), (2 * NC) ** -0.5, 1.5, ((0, 8), (2, 16)), jnp.float32)
    kspace = normal_values(arg_keys[1], (NC, 2, NX, NY, NZ), 1.0, 6.0, ((0, 8), (2, 16)), jnp.float32)
    sample_mask = with_ends((jax.random.randint(arg_keys[2], (NY, NZ), 0, 3) < 1).astype(jnp.int32), jax.random.fold_in(arg_keys[2], 1), 0, 1)
    iterate = normal_values(arg_keys[3], (2, NX, NY, NZ), 1.0, 6.0, ((1, 16), (2, 8)), jnp.float32)
    probe_bits = with_ends(jax.random.randint(arg_keys[4], (2, NX, NY, NZ), 0, 2), jax.random.fold_in(arg_keys[4], 1), 0, 1).astype(jnp.int32)
    loss_gradient = normal_values(arg_keys[5], (2, NX, NY, NZ), 1.0, 6.0, ((1, 16), (2, 8)), jnp.float32)
    adjoint = normal_values(arg_keys[6], (2, NX, NY, NZ), 1.0, 6.0, ((1, 16), (2, 8)), jnp.float32)
    kernel_first = normal_values(arg_keys[7], (CH, 2, 3, 3, 3), 54 ** -0.5, 0.875)
    kernel_second = normal_values(arg_keys[8], (CH, CH, 3, 3, 3), (27 * CH) ** -0.5, 0.25)
    kernel_last = normal_values(arg_keys[9], (2, CH, 3, 3, 3), (27 * CH) ** -0.5, 0.25)
    return {"coil_maps": coil_maps, "kspace": kspace, "sample_mask": sample_mask, "iterate": iterate, "probe_bits": probe_bits, "loss_gradient": loss_gradient, "adjoint": adjoint, "kernel_first": kernel_first, "kernel_second": kernel_second, "kernel_last": kernel_last}


step_size = 0.8
kernel_layout = ("NCDHW", "OIDHW", "NCDHW")


def spectrum(real_part, imag_part, inverse):
    joined = lax.complex(real_part, imag_part)
    if inverse:
        turned = jnp.fft.ifft2(joined, axes=(-2, -1), norm="ortho")
    else:
        turned = jnp.fft.fft2(joined, axes=(-2, -1), norm="ortho")
    return jnp.real(turned), jnp.imag(turned)


def coil_term(field, coil_map, mask_weight, data):
    field_real = field[:, 0]
    field_imag = field[:, 1]
    map_real = coil_map[0]
    map_imag = coil_map[1]
    coil_real = map_real * field_real - map_imag * field_imag
    coil_imag = map_real * field_imag + map_imag * field_real
    freq_real, freq_imag = spectrum(coil_real, coil_imag, False)
    freq_real = mask_weight * freq_real
    freq_imag = mask_weight * freq_imag
    if data is not None:
        freq_real = freq_real - mask_weight * data[0]
        freq_imag = freq_imag - mask_weight * data[1]
    back_real, back_imag = spectrum(freq_real, freq_imag, True)
    return jnp.stack([map_real * back_real + map_imag * back_imag,
                      map_real * back_imag - map_imag * back_real], axis=1)


def normal_sum(field, coil_maps, kspace, mask_weight, with_data):
    def coil_step(running, coil_index):
        data = kspace[coil_index] if with_data else None
        return running + coil_term(field, coil_maps[coil_index], mask_weight, data), None

    running, unused = lax.scan(coil_step, jnp.zeros(field.shape, jnp.float32),
                               jnp.arange(NC, dtype=jnp.int32))
    return running


def convolve(activation, kernel):
    return lax.conv_general_dilated(activation, kernel, (1, 1, 1), "SAME",
                                    dimension_numbers=kernel_layout,
                                    preferred_element_type=jnp.float32)


def transposed(kernel):
    return jnp.swapaxes(jnp.flip(kernel, (2, 3, 4)), 0, 1)


def silu_slope(preact):
    sigmoid_value = jax.nn.sigmoid(preact)
    return sigmoid_value * (1.0 + preact * (1.0 - sigmoid_value))


def reference(coil_maps, kspace, sample_mask, iterate, probe_bits, loss_gradient, adjoint,
              kernel_first, kernel_second, kernel_last):
    mask_weight = sample_mask.astype(jnp.float32)
    gradient = normal_sum(iterate[None], coil_maps, kspace, mask_weight, True)[0]
    relaxed = iterate - step_size * gradient
    activation = relaxed.astype(jnp.bfloat16)[None]
    preacts = []
    for kernel in (kernel_first, kernel_second):
        preact = convolve(activation, kernel)
        preacts.append(preact)
        activation = jax.nn.silu(preact).astype(jnp.bfloat16)
    new_iterate = relaxed + convolve(activation, kernel_last)[0]

    def pullback(cotangent):
        grad_field = convolve(cotangent.astype(jnp.bfloat16)[None], transposed(kernel_last))
        for kernel, preact in ((kernel_second, preacts[1]), (kernel_first, preacts[0])):
            grad_field = (grad_field * silu_slope(preact)).astype(jnp.bfloat16)
            grad_field = convolve(grad_field, transposed(kernel))
        return cotangent + grad_field[0]

    sign_field = (2 * probe_bits - 1).astype(jnp.float32)
    pulled = jnp.stack([pullback(sign_field), pullback(adjoint)])
    result = pulled - step_size * normal_sum(pulled, coil_maps, kspace, mask_weight, False)
    return new_iterate, result[0], loss_gradient + result[1]
```

```python
import math

import jax
import jax.numpy as jnp
import numpy as np
from jax import lax
from jax.experimental import pallas as pl
from jax.experimental.pallas import tpu as pltpu
from jax.sharding import PartitionSpec as P

STEP = 0.8
F32 = jnp.float32
BF16 = jnp.bfloat16
NZ = 128
NY = 256
NYL = 32
HALO_ROWS = 40
VMEM_BIG = 56 << 20


def whole(count):
    return [pl.BlockSpec(memory_space=pltpu.VMEM)] * count


def split_host(table):
    high = table.astype(np.float32).astype(jnp.bfloat16)
    low = (table - high.astype(np.float64)).astype(jnp.bfloat16)
    return high, low


def fourier_constants():
    def cos_sin(length):
        index = np.arange(length)
        angles = (index[:, None] * index[None, :] % length) * (2.0 * math.pi / length)
        return np.cos(angles) / math.sqrt(length), np.sin(angles) / math.sqrt(length)

    cos_y, sin_y = cos_sin(NY)
    cos_z, sin_z = cos_sin(NZ)
    along_y = np.concatenate([cos_y, sin_y], axis=0)
    along_z = np.block([[cos_z, -sin_z], [sin_z, cos_z]])
    return split_host(along_y) + split_host(along_z)


def split(values):
    high = values.astype(BF16)
    return high, (values - high.astype(F32)).astype(BF16)


def mm(left, right):
    return jnp.dot(left, right, preferred_element_type=F32)


def along_z(joined, high_ref, low_ref):
    high, low = split(joined)
    return mm(high, high_ref[...]) + (mm(high, low_ref[...]) + mm(low, high_ref[...]))


def along_y(joined, high_ref, low_ref):
    high, low = split(joined)
    return mm(high_ref[...], high) + (mm(low_ref[...], high) + mm(high_ref[...], low))


def forward(real, imag, tabs):
    y_high, y_low, z_high, z_low = tabs
    turned = along_y(along_z(jnp.concatenate([real, imag], 1), z_high, z_low), y_high, y_low)
    cos_part, sin_part = turned[:NY], turned[NY:]
    return cos_part[:, :NZ] + sin_part[:, NZ:], cos_part[:, NZ:] - sin_part[:, :NZ]


def inverse(real, imag, tabs):
    y_high, y_low, z_high, z_low = tabs
    turned = along_y(jnp.concatenate([real, imag], 1), y_high, y_low)
    cos_part, sin_part = turned[:NY], turned[NY:]
    back = cos_part[:, :NZ] - sin_part[:, NZ:], -(cos_part[:, NZ:] + sin_part[:, :NZ])
    turned = along_z(jnp.concatenate(back, 1), z_high, z_low)
    return turned[:, :NZ], -turned[:, NZ:]


def gradient_kernel(
    field_ref, maps_ref, kspace_ref, mask_ref, bits_ref, adj_ref, yh, yl, zh, zl, out_ref, pad
):
    tabs = (yh, yl, zh, zl)
    weight = mask_ref[...].astype(F32)
    map_re, map_im = maps_ref[0], maps_ref[1]
    re = field_ref[:, 0].reshape(NY, NZ)
    im = field_ref[:, 1].reshape(NY, NZ)
    f_re, f_im = forward(map_re * re - map_im * im, map_re * im + map_im * re, tabs)
    f_re = weight * (f_re - kspace_ref[0])
    f_im = weight * (f_im - kspace_ref[1])
    b_re, b_im = inverse(f_re, f_im, tabs)
    zero = jnp.zeros((4, NZ), F32)
    for ch in range(2):
        pad[ch, 0:4] = zero
        pad[ch, NY + 4 : NY + 8] = zero
    pad[0, 4 : NY + 4] = map_re * b_re + map_im * b_im
    pad[1, 4 : NY + 4] = map_re * b_im - map_im * b_re
    edges = []
    for ch in range(4):
        if ch < 2:
            rows = (2 * bits_ref[ch] - 1).astype(F32)
        else:
            rows = adj_ref[ch - 2]
        edges += [rows[0:4], rows[NYL - 4 : NYL]]
    edges = jnp.concatenate(edges + [jnp.zeros((8, NZ), F32)], 0).astype(BF16)
    for dest in range(8):
        for ch in range(2):
            out_ref[dest, ch] = pad[ch, NYL * dest : NYL * dest + HALO_ROWS].astype(BF16)
        out_ref[dest, 2] = edges


def relax_kernel(place_ref, got_ref, field_ref, bits_ref, adj_ref, out_ref, relaxed_ref, pad, qpad):
    coil = place_ref[0]
    zero = jnp.zeros((4, NZ), F32)
    first = pl.multiple_of(coil * NYL, NYL)
    for ch in range(2):
        pad[ch, 0:4] = zero
        pad[ch, NY + 4 : NY + 8] = zero
        pad[ch, 4 : NY + 4] = field_ref[:, ch].reshape(NY, NZ)
        total = got_ref[0, ch].astype(F32)
        for source in range(1, 8):
            total = total + got_ref[source, ch].astype(F32)
        relaxed = pad[ch, pl.ds(first, HALO_ROWS)] - STEP * total
        relaxed_ref[ch] = relaxed[4 : 4 + NYL]
        rows = relaxed.astype(BF16)
        for dest in range(16):
            out_ref[dest, ch] = rows
    below = got_ref[jnp.maximum(coil - 1, 0), 2].astype(F32)
    above = got_ref[jnp.minimum(coil + 1, 7), 2].astype(F32)
    below = jnp.where(coil > 0, below, 0.0)
    above = jnp.where(coil < 7, above, 0.0)
    for ch in range(4):
        if ch < 2:
            rows = (2 * bits_ref[ch] - 1).astype(F32)
        else:
            rows = adj_ref[ch - 2]
        qpad[ch, 0:3] = below[ch * 8 + 5 : ch * 8 + 8]
        qpad[ch, 3 : 3 + NYL] = rows
        qpad[ch, 3 + NYL : 7 + NYL] = above[ch * 8 : ch * 8 + 4]
        qpad[ch, 7 + NYL : HALO_ROWS] = zero[0:1]
        packed = qpad[ch].astype(BF16)
        for dest in range(16):
            out_ref[dest, 2 + ch] = packed


def dot_first(left, right):
    return lax.dot_general(left, right, (((0,), (0,)), ((), ())), preferred_element_type=F32)


def tables_kernel(k1_ref, k2_ref, k3_ref, t1_ref, t2_ref, t3_ref, t1t_ref, t2t_ref, t3t_ref):
    lane = lax.broadcasted_iota(jnp.int32, (24, 256), 1)
    row = lax.broadcasted_iota(jnp.int32, (24, 256), 0)
    tile24 = ((lane % 24 == row) & (lane < 240)).astype(BF16)
    window = jnp.where(lane < 240, lane // 24, 99)

    def tap(dx, dy, dz, flip):
        if flip:
            dx, dy, dz = 2 - dx, 2 - dy, 2 - dz
        return dx * 9 + dy * 3 + dz

    for target, flip in ((t2_ref, False), (t2t_ref, True)):
        for dz in range(3):
            for dx in range(3):
                spread = []
                for dy in range(3):
                    block = k2_ref[tap(dx, dy, dz, flip)]
                    spread.append(dot_first(block, tile24) if flip else mm(block, tile24))
                for yo in range(8):
                    value = jnp.zeros((24, 256), F32)
                    for dy in range(3):
                        value = jnp.where(window == yo + dy, spread[dy], value)
                    at = dz * 192 + yo * 24
                    target[at : at + 24, dx * 256 : dx * 256 + 256] = value.astype(BF16)

    lane96 = lax.broadcasted_iota(jnp.int32, (24, 96), 1)
    lane2 = lax.broadcasted_iota(jnp.int32, (2, 96), 1)
    row2 = lax.broadcasted_iota(jnp.int32, (2, 96), 0)
    tile2 = ((lane2 // 16) % 2 == row2).astype(BF16)
    code = (lane96 // 32) * 16 + lane96 % 16
    for target, source, flip in ((t1_ref, k1_ref, False), (t3t_ref, k3_ref, True)):
        for dz in range(3):
            spread = {}
            for dx in range(3):
                for dy in range(3):
                    spread[dx, dy] = dot_first(source[tap(dx, dy, dz, flip)], tile2)
            for yo in range(8):
                value = jnp.zeros((24, 96), F32)
                for dx in range(3):
                    for dy in range(3):
                        value = jnp.where(code == dx * 16 + yo + dy, spread[dx, dy], value)
                at = dz * 192 + yo * 24
                target[at : at + 24, :] = value.astype(BF16)

    window8 = window[0:8] - lax.broadcasted_iota(jnp.int32, (8, 256), 0)
    for target, source, flip in ((t3_ref, k3_ref, False), (t1t_ref, k1_ref, True)):
        for dz in range(3):
            for dx in range(3):
                spread = [mm(source[tap(dx, dy, dz, flip)], tile24) for dy in range(3)]
                both = []
                for ch in range(2):
                    value = jnp.zeros((8, 256), F32)
                    for dy in range(3):
                        value = jnp.where(window8 == dy, spread[dy][ch : ch + 1], value)
                    both.append(value)
                target[dz * 16 : dz * 16 + 16, dx * 256 : dx * 256 + 256] = jnp.concatenate(
                    both, 0
                ).astype(BF16)


def tables(kernel_first, kernel_second, kernel_last):
    k1 = jnp.transpose(kernel_first, (2, 3, 4, 1, 0)).reshape(27, 2, 24)
    k2 = jnp.transpose(kernel_second, (2, 3, 4, 0, 1)).reshape(27, 24, 24)
    k3 = jnp.transpose(kernel_last, (2, 3, 4, 0, 1)).reshape(27, 2, 24)
    shapes = [(576, 96), (576, 768), (48, 768), (48, 768), (576, 768), (576, 96)]
    return pl.pallas_call(
        tables_kernel,
        out_shape=[jax.ShapeDtypeStruct(s, BF16) for s in shapes],
        in_specs=whole(3),
        out_specs=whole(6),
        cost_estimate=pl.CostEstimate(flops=10**9, bytes_accessed=4 * 10**6, transcendentals=0),
    )(k1, k2, k3)


def join_z(parts, rows, half, at_low, at_high):
    lanes = slice(half * NZ, half * NZ + NZ)
    before = jnp.where(at_low, 0.0, pltpu.roll(parts[0:rows, lanes], 1, 1))
    after = jnp.where(at_high, 0.0, pltpu.roll(parts[2 * rows : 3 * rows, lanes], NZ - 1, 1))
    return parts[rows : 2 * rows, lanes] + (before + after)


def denoise_kernel(
    place_ref,
    planes_ref,
    relaxed_ref,
    bits_ref,
    adj_ref,
    t1_ref,
    t2_ref,
    t3_ref,
    t1t_ref,
    t2t_ref,
    t3t_ref,
    new_ref,
    pulled_ref,
    send_ref,
    image,
    cots,
    a1,
    s1,
    a2,
    e2,
    e1,
):
    coil, slab = place_ref[0], place_ref[1]
    tail8 = jnp.zeros((8, NZ), F32)

    def inside(plane):
        return (plane >= 0) & (plane < 16)

    for j in range(10):
        plane = slab - 4 + j
        keep = inside(plane) & (j < 9)
        source = jnp.clip(plane, 0, 15)
        for ch in range(2):
            image[j, ch, 0:HALO_ROWS] = jnp.where(keep, planes_ref[source, ch].astype(F32), 0.0)
            image[j, ch, HALO_ROWS:48] = tail8
        if 1 <= j < 9:
            for ch in range(4):
                cots[j - 1, ch, 0:HALO_ROWS] = jnp.where(
                    keep, planes_ref[source, 2 + ch].astype(F32), 0.0
                )
                cots[j - 1, ch, HALO_ROWS:48] = tail8

    def at_edges(rows):
        column = lax.broadcasted_iota(jnp.int32, (rows, NZ), 1)
        return column == 0, column == NZ - 1

    low, high = at_edges(192)
    zero64 = jnp.zeros((64, NZ), BF16)
    for j in range(8):
        a1[j, 960:1024] = zero64
        s1[j, 960:1024] = jnp.zeros((64, NZ), F32)
    for j in range(6):
        a2[j, 960:1024] = zero64
        e2[j, 960:1024] = jnp.zeros((64, 2 * NZ), BF16)
    for j in range(3):
        e1[j, 960:1024] = jnp.zeros((64, 2 * NZ), BF16)

    def first_step(step, carry):
        pair, block = 2 * (step // 5), step % 5
        at = pl.multiple_of(8 * block, 8)
        to = pl.multiple_of(192 * block, 192)
        pieces = []
        for dx in range(3):
            for ch in range(2):
                pieces.append(
                    jnp.concatenate(
                        [
                            image[pair + dx, ch, pl.ds(at, 16)],
                            image[pair + dx + 1, ch, pl.ds(at, 16)],
                        ],
                        1,
                    ).astype(BF16)
                )
        parts = mm(t1_ref[...], jnp.concatenate(pieces, 0))
        for half in range(2):
            pre = join_z(parts, 192, half, low, high)
            gate = jax.nn.sigmoid(pre)
            a1[pair + half, pl.ds(to, 192)] = (pre * gate).astype(BF16)
            s1[pair + half, pl.ds(to, 192)] = gate * (1.0 + pre * (1.0 - gate))
        return carry

    lax.fori_loop(0, 20, first_step, 0)

    def clear(ref, planes, offset, top, bottom, width):
        for j in range(planes):

            @pl.when(jnp.logical_not(inside(slab + offset + j)))
            def _():
                ref[j] = jnp.zeros((1024, width), BF16)

        @pl.when(coil == 0)
        def _():
            for j in range(planes):
                ref[j, 0:top] = jnp.zeros((top, width), BF16)

        @pl.when(coil == 7)
        def _():
            for j in range(planes):
                ref[j, bottom:1024] = jnp.zeros((1024 - bottom, width), BF16)

    clear(a1, 8, -3, 72, 840, NZ)

    def second_step(step, carry):
        pair, block = 2 * (step // 5), step % 5
        at = pl.multiple_of(8 * block, 8)
        to = pl.multiple_of(192 * block, 192)
        stacked = jnp.concatenate(
            [
                jnp.concatenate(
                    [a1[pair + dx, pl.ds(to, 256)], a1[pair + dx + 1, pl.ds(to, 256)]], 1
                )
                for dx in range(3)
            ],
            0,
        )
        parts = mm(t2_ref[...], stacked)
        for half in range(2):
            pre = join_z(parts, 192, half, low, high)
            gate = jax.nn.sigmoid(pre)
            a2[pair + half, pl.ds(to, 192)] = (pre * gate).astype(BF16)
            slope = gate * (1.0 + pre * (1.0 - gate))
            pieces = []
            for dx in range(3):
                for ch in range(2):
                    pieces.append(
                        jnp.concatenate(
                            [
                                cots[pair + half + dx, ch, pl.ds(at, 16)],
                                cots[pair + half + dx, 2 + ch, pl.ds(at, 16)],
                            ],
                            1,
                        ).astype(BF16)
                    )
            back = mm(t3t_ref[...], jnp.concatenate(pieces, 0))
            for which in range(2):
                grad = join_z(back, 192, which, low, high) * slope
                e2[pair + half, pl.ds(to, 192), which * NZ : which * NZ + NZ] = grad.astype(BF16)
        return carry

    lax.fori_loop(0, 15, second_step, 0)
    clear(a2, 6, -2, 48, 816, NZ)
    clear(e2, 6, -2, 48, 816, 2 * NZ)

    def third_step(step, carry):
        plane, block = step // 5, step % 5
        to = pl.multiple_of(192 * block, 192)
        stacked = jnp.concatenate([e2[plane + dx, pl.ds(to, 256)] for dx in range(3)], 0)
        back = mm(t2t_ref[...], stacked)
        slope = s1[plane + 2, pl.ds(to + 48, 192)]
        for which in range(2):
            grad = join_z(back, 192, which, low, high) * slope
            e1[plane, pl.ds(to, 192), which * NZ : which * NZ + NZ] = grad.astype(BF16)
        return carry

    lax.fori_loop(0, 15, third_step, 0)
    clear(e1, 3, -1, 24, 792, 2 * NZ)

    low16, high16 = at_edges(16)
    for pair in range(2):
        stacked = jnp.concatenate(
            [
                jnp.concatenate(
                    [
                        a2[1 + dx, 24 + 384 * pair : 280 + 384 * pair],
                        a2[1 + dx, 216 + 384 * pair : 472 + 384 * pair],
                    ],
                    1,
                )
                for dx in range(3)
            ],
            0,
        )
        parts = mm(t3_ref[...], stacked)
        for half in range(2):
            update = join_z(parts, 16, half, low16, high16)
            at = 16 * pair + 8 * half
            for ch in range(2):
                new_ref[ch, at : at + 8] = (
                    relaxed_ref[ch, at : at + 8] + update[8 * ch : 8 * ch + 8]
                )

    for block in range(4):
        stacked = jnp.concatenate([e1[dx, 192 * block : 192 * block + 256] for dx in range(3)], 0)
        back = mm(t1t_ref[...], stacked)
        for which in range(2):
            grad = join_z(back, 16, which, low16, high16)
            for ch in range(2):
                rows = slice(8 * block, 8 * block + 8)
                if which == 0:
                    base = (2 * bits_ref[ch, rows] - 1).astype(F32)
                else:
                    base = adj_ref[ch, rows]
                pulled_ref[2 * which + ch, rows] = base + grad[8 * ch : 8 * ch + 8]
    for ch in range(4):
        rows = pulled_ref[ch].astype(BF16)
        for dest in range(8):
            send_ref[dest, ch] = rows


def normal_kernel(field_ref, maps_ref, mask_ref, yh, yl, zh, zl, out_ref):
    tabs = (yh, yl, zh, zl)
    weight = mask_ref[...].astype(F32)
    map_re, map_im = maps_ref[0], maps_ref[1]
    for which in range(2):
        re = field_ref[:, 2 * which].reshape(NY, NZ).astype(F32)
        im = field_ref[:, 2 * which + 1].reshape(NY, NZ).astype(F32)
        f_re, f_im = forward(map_re * re - map_im * im, map_re * im + map_im * re, tabs)
        b_re, b_im = inverse(weight * f_re, weight * f_im, tabs)
        out_re = (map_re * b_re + map_im * b_im).astype(BF16)
        out_im = (map_re * b_im - map_im * b_re).astype(BF16)
        for dest in range(8):
            rows = slice(NYL * dest, NYL * dest + NYL)
            out_ref[dest, 2 * which] = out_re[rows]
            out_ref[dest, 2 * which + 1] = out_im[rows]


def final_kernel(got_ref, pulled_ref, loss_ref, probe_ref, next_ref):
    for ch in range(4):
        total = got_ref[0, ch].astype(F32)
        for source in range(1, 8):
            total = total + got_ref[source, ch].astype(F32)
        result = pulled_ref[ch] - STEP * total
        if ch < 2:
            probe_ref[ch] = result
        else:
            next_ref[ch - 2] = loss_ref[ch - 2] + result


def on_device(
    coil_maps,
    kspace,
    sample_mask,
    iterate,
    probe_bits,
    loss_gradient,
    adjoint,
    kernel_first,
    kernel_second,
    kernel_last,
):
    maps = coil_maps[0, :, 0]
    data = kspace[0, :, 0]
    iterate, bits, loss, adj = (
        a[:, 0] for a in (iterate, probe_bits, loss_gradient, adjoint)
    )
    fourier = [jnp.asarray(t) for t in fourier_constants()]
    place = jnp.stack([lax.axis_index("coil"), lax.axis_index("slab")]).astype(jnp.int32)
    smem = pl.BlockSpec(memory_space=pltpu.SMEM)

    toeplitz = tables(kernel_first, kernel_second, kernel_last)
    field = lax.all_to_all(jnp.broadcast_to(iterate[None], (8,) + iterate.shape), "coil", 0, 0)
    partial_sums = pl.pallas_call(
        gradient_kernel,
        out_shape=jax.ShapeDtypeStruct((8, 3, HALO_ROWS, NZ), BF16),
        in_specs=whole(10),
        out_specs=whole(1)[0],
        scratch_shapes=[pltpu.VMEM((2, NY + 8, NZ), F32)],
    )(field, maps, data, sample_mask, bits, adj, *fourier)
    got = lax.all_to_all(partial_sums, "coil", 0, 0)
    payload, relaxed = pl.pallas_call(
        relax_kernel,
        out_shape=[
            jax.ShapeDtypeStruct((16, 6, HALO_ROWS, NZ), BF16),
            jax.ShapeDtypeStruct((2, NYL, NZ), F32),
        ],
        in_specs=[smem] + whole(4),
        out_specs=whole(2),
        scratch_shapes=[pltpu.VMEM((2, NY + 8, NZ), F32), pltpu.VMEM((4, HALO_ROWS, NZ), F32)],
    )(place, got, field, bits, adj)
    planes = lax.all_to_all(payload, "slab", 0, 0)
    new_iterate, pulled, send = pl.pallas_call(
        denoise_kernel,
        out_shape=[
            jax.ShapeDtypeStruct((2, NYL, NZ), F32),
            jax.ShapeDtypeStruct((4, NYL, NZ), F32),
            jax.ShapeDtypeStruct((8, 4, NYL, NZ), BF16),
        ],
        in_specs=[smem] + whole(10),
        out_specs=whole(3),
        scratch_shapes=[
            pltpu.VMEM((10, 2, 48, NZ), F32),
            pltpu.VMEM((8, 4, 48, NZ), F32),
            pltpu.VMEM((8, 1024, NZ), BF16),
            pltpu.VMEM((8, 1024, NZ), F32),
            pltpu.VMEM((6, 1024, NZ), BF16),
            pltpu.VMEM((6, 1024, 2 * NZ), BF16),
            pltpu.VMEM((3, 1024, 2 * NZ), BF16),
        ],
        compiler_params=pltpu.CompilerParams(vmem_limit_bytes=VMEM_BIG),
    )(place, planes, relaxed, bits, adj, *toeplitz)
    spread = lax.all_to_all(send, "coil", 0, 0)
    back = pl.pallas_call(
        normal_kernel,
        out_shape=jax.ShapeDtypeStruct((8, 4, NYL, NZ), BF16),
        in_specs=whole(7),
        out_specs=whole(1)[0],
    )(spread, maps, sample_mask, *fourier)
    back = lax.all_to_all(back, "coil", 0, 0)
    probe, following = pl.pallas_call(
        final_kernel,
        out_shape=[jax.ShapeDtypeStruct((2, NYL, NZ), F32)] * 2,
        in_specs=whole(3),
        out_specs=whole(2),
    )(back, pulled, loss)
    return new_iterate[:, None], probe[:, None], following[:, None]


def solution(mesh):
    image = P(None, "slab", "coil", None)
    coils = P("coil", None, "slab", None, None)
    return jax.shard_map(
        on_device,
        mesh=mesh,
        in_specs=(coils, coils, P(), image, image, image, image, P(), P(), P()),
        out_specs=(image, image, image),
        check_vma=False,
    )
```

```python
import math

import jax
import jax.numpy as jnp
import numpy as np
from jax import lax
from jax.experimental import pallas as pl
from jax.experimental.pallas import tpu as pltpu
from jax.sharding import PartitionSpec as P

STEP = 0.8
F32 = jnp.float32
BF16 = jnp.bfloat16
NZ = 128
NY = 256
NYL = 32
HALO_ROWS = 40
VMEM_BIG = 56 << 20


def whole(count):
    return [pl.BlockSpec(memory_space=pltpu.VMEM)] * count


def split_host(table):
    high = table.astype(np.float32).astype(jnp.bfloat16)
    low = (table - high.astype(np.float64)).astype(jnp.bfloat16)
    return high, low


def fourier_constants():
    def cos_sin(length):
        index = np.arange(length)
        angles = (index[:, None] * index[None, :] % length) * (2.0 * math.pi / length)
        return np.cos(angles) / math.sqrt(length), np.sin(angles) / math.sqrt(length)

    cos_y, sin_y = cos_sin(NY)
    cos_z, sin_z = cos_sin(NZ)
    along_y = np.concatenate([cos_y, sin_y], axis=0)
    along_z = np.block([[cos_z, -sin_z], [sin_z, cos_z]])
    return split_host(along_y) + split_host(along_z)


def split(values):
    high = values.astype(BF16)
    return high, (values - high.astype(F32)).astype(BF16)


def mm(left, right):
    return jnp.dot(left, right, preferred_element_type=F32)


def along_z(joined, high_ref, low_ref):
    high, low = split(joined)
    return mm(high, high_ref[...]) + (mm(high, low_ref[...]) + mm(low, high_ref[...]))


def along_y(joined, high_ref, low_ref):
    high, low = split(joined)
    return mm(high_ref[...], high) + (mm(low_ref[...], high) + mm(high_ref[...], low))


def forward(real, imag, tabs):
    y_high, y_low, z_high, z_low = tabs
    turned = along_y(along_z(jnp.concatenate([real, imag], 1), z_high, z_low), y_high, y_low)
    cos_part, sin_part = turned[:NY], turned[NY:]
    return cos_part[:, :NZ] + sin_part[:, NZ:], cos_part[:, NZ:] - sin_part[:, :NZ]


def inverse(real, imag, tabs):
    y_high, y_low, z_high, z_low = tabs
    turned = along_y(jnp.concatenate([real, imag], 1), y_high, y_low)
    cos_part, sin_part = turned[:NY], turned[NY:]
    back = cos_part[:, :NZ] - sin_part[:, NZ:], -(cos_part[:, NZ:] + sin_part[:, :NZ])
    turned = along_z(jnp.concatenate(back, 1), z_high, z_low)
    return turned[:, :NZ], -turned[:, NZ:]


def gradient_kernel(
    field_ref, maps_ref, kspace_ref, mask_ref, bits_ref, adj_ref, yh, yl, zh, zl, out_ref, pad
):
    tabs = (yh, yl, zh, zl)
    weight = mask_ref[...].astype(F32)
    map_re, map_im = maps_ref[0], maps_ref[1]
    re = field_ref[:, 0].reshape(NY, NZ)
    im = field_ref[:, 1].reshape(NY, NZ)
    f_re, f_im = forward(map_re * re - map_im * im, map_re * im + map_im * re, tabs)
    f_re = weight * (f_re - kspace_ref[0])
    f_im = weight * (f_im - kspace_ref[1])
    b_re, b_im = inverse(f_re, f_im, tabs)
    zero = jnp.zeros((4, NZ), F32)
    for ch in range(2):
        pad[ch, 0:4] = zero
        pad[ch, NY + 4 : NY + 8] = zero
    pad[0, 4 : NY + 4] = map_re * b_re + map_im * b_im
    pad[1, 4 : NY + 4] = map_re * b_im - map_im * b_re
    edges = []
    for ch in range(4):
        if ch < 2:
            rows = (2 * bits_ref[ch] - 1).astype(F32)
        else:
            rows = adj_ref[ch - 2]
        edges += [rows[0:4], rows[NYL - 4 : NYL]]
    edges = jnp.concatenate(edges + [jnp.zeros((8, NZ), F32)], 0).astype(BF16)
    for dest in range(8):
        for ch in range(2):
            out_ref[dest, ch] = pad[ch, NYL * dest : NYL * dest + HALO_ROWS].astype(BF16)
        out_ref[dest, 2] = edges


def relax_kernel(place_ref, got_ref, field_ref, bits_ref, adj_ref, out_ref, relaxed_ref, pad, qpad):
    coil = place_ref[0]
    zero = jnp.zeros((4, NZ), F32)
    first = pl.multiple_of(coil * NYL, NYL)
    for ch in range(2):
        pad[ch, 0:4] = zero
        pad[ch, NY + 4 : NY + 8] = zero
        pad[ch, 4 : NY + 4] = field_ref[:, ch].reshape(NY, NZ)
        total = got_ref[0, ch].astype(F32)
        for source in range(1, 8):
            total = total + got_ref[source, ch].astype(F32)
        relaxed = pad[ch, pl.ds(first, HALO_ROWS)] - STEP * total
        relaxed_ref[ch] = relaxed[4 : 4 + NYL]
        rows = relaxed.astype(BF16)
        for dest in range(16):
            out_ref[dest, ch] = rows
    below = got_ref[jnp.maximum(coil - 1, 0), 2].astype(F32)
    above = got_ref[jnp.minimum(coil + 1, 7), 2].astype(F32)
    below = jnp.where(coil > 0, below, 0.0)
    above = jnp.where(coil < 7, above, 0.0)
    for ch in range(4):
        if ch < 2:
            rows = (2 * bits_ref[ch] - 1).astype(F32)
        else:
            rows = adj_ref[ch - 2]
        qpad[ch, 0:3] = below[ch * 8 + 5 : ch * 8 + 8]
        qpad[ch, 3 : 3 + NYL] = rows
        qpad[ch, 3 + NYL : 7 + NYL] = above[ch * 8 : ch * 8 + 4]
        qpad[ch, 7 + NYL : HALO_ROWS] = zero[0:1]
        packed = qpad[ch].astype(BF16)
        for dest in range(16):
            out_ref[dest, 2 + ch] = packed


def dot_first(left, right):
    return lax.dot_general(left, right, (((0,), (0,)), ((), ())), preferred_element_type=F32)


def tables_kernel(k1_ref, k2_ref, k3_ref, t1_ref, t2_ref, t3_ref, t1t_ref, t2t_ref, t3t_ref):
    lane = lax.broadcasted_iota(jnp.int32, (24, 256), 1)
    row = lax.broadcasted_iota(jnp.int32, (24, 256), 0)
    tile24 = ((lane % 24 == row) & (lane < 240)).astype(BF16)
    window = jnp.where(lane < 240, lane // 24, 99)

    def tap(dx, dy, dz, flip):
        if flip:
            dx, dy, dz = 2 - dx, 2 - dy, 2 - dz
        return dx * 9 + dy * 3 + dz

    for target, flip in ((t2_ref, False), (t2t_ref, True)):
        for dz in range(3):
            for dx in range(3):
                spread = []
                for dy in range(3):
                    block = k2_ref[tap(dx, dy, dz, flip)]
                    spread.append(dot_first(block, tile24) if flip else mm(block, tile24))
                for yo in range(8):
                    value = jnp.zeros((24, 256), F32)
                    for dy in range(3):
                        value = jnp.where(window == yo + dy, spread[dy], value)
                    at = dz * 192 + yo * 24
                    target[at : at + 24, dx * 256 : dx * 256 + 256] = value.astype(BF16)

    lane96 = lax.broadcasted_iota(jnp.int32, (24, 96), 1)
    lane2 = lax.broadcasted_iota(jnp.int32, (2, 96), 1)
    row2 = lax.broadcasted_iota(jnp.int32, (2, 96), 0)
    tile2 = ((lane2 // 16) % 2 == row2).astype(BF16)
    code = (lane96 // 32) * 16 + lane96 % 16
    for target, source, flip in ((t1_ref, k1_ref, False), (t3t_ref, k3_ref, True)):
        for dz in range(3):
            spread = {}
            for dx in range(3):
                for dy in range(3):
                    spread[dx, dy] = dot_first(source[tap(dx, dy, dz, flip)], tile2)
            for yo in range(8):
                value = jnp.zeros((24, 96), F32)
                for dx in range(3):
                    for dy in range(3):
                        value = jnp.where(code == dx * 16 + yo + dy, spread[dx, dy], value)
                at = dz * 192 + yo * 24
                target[at : at + 24, :] = value.astype(BF16)

    window8 = window[0:8] - lax.broadcasted_iota(jnp.int32, (8, 256), 0)
    for target, source, flip in ((t3_ref, k3_ref, False), (t1t_ref, k1_ref, True)):
        for dz in range(3):
            for dx in range(3):
                spread = [mm(source[tap(dx, dy, dz, flip)], tile24) for dy in range(3)]
                both = []
                for ch in range(2):
                    value = jnp.zeros((8, 256), F32)
                    for dy in range(3):
                        value = jnp.where(window8 == dy, spread[dy][ch : ch + 1], value)
                    both.append(value)
                target[dz * 16 : dz * 16 + 16, dx * 256 : dx * 256 + 256] = jnp.concatenate(
                    both, 0
                ).astype(BF16)


def tables(kernel_first, kernel_second, kernel_last):
    k1 = jnp.transpose(kernel_first, (2, 3, 4, 1, 0)).reshape(27, 2, 24)
    k2 = jnp.transpose(kernel_second, (2, 3, 4, 0, 1)).reshape(27, 24, 24)
    k3 = jnp.transpose(kernel_last, (2, 3, 4, 0, 1)).reshape(27, 2, 24)
    shapes = [(576, 96), (576, 768), (48, 768), (48, 768), (576, 768), (576, 96)]
    return pl.pallas_call(
        tables_kernel,
        out_shape=[jax.ShapeDtypeStruct(s, BF16) for s in shapes],
        in_specs=whole(3),
        out_specs=whole(6),
        cost_estimate=pl.CostEstimate(flops=10**9, bytes_accessed=4 * 10**6, transcendentals=0),
    )(k1, k2, k3)


def join_z(parts, rows, half, at_low, at_high):
    lanes = slice(half * NZ, half * NZ + NZ)
    before = jnp.where(at_low, 0.0, pltpu.roll(parts[0:rows, lanes], 1, 1))
    after = jnp.where(at_high, 0.0, pltpu.roll(parts[2 * rows : 3 * rows, lanes], NZ - 1, 1))
    return parts[rows : 2 * rows, lanes] + (before + after)


def denoise_kernel(
    place_ref,
    planes_ref,
    relaxed_ref,
    bits_ref,
    adj_ref,
    t1_ref,
    t2_ref,
    t3_ref,
    t1t_ref,
    t2t_ref,
    t3t_ref,
    new_ref,
    pulled_ref,
    send_ref,
    image,
    cots,
    a1,
    s1,
    a2,
    e2,
    e1,
):
    coil, slab = place_ref[0], place_ref[1]
    tail8 = jnp.zeros((8, NZ), F32)

    def inside(plane):
        return (plane >= 0) & (plane < 16)

    for j in range(10):
        plane = slab - 4 + j
        keep = inside(plane) & (j < 9)
        source = jnp.clip(plane, 0, 15)
        for ch in range(2):
            image[j, ch, 0:HALO_ROWS] = jnp.where(keep, planes_ref[source, ch].astype(F32), 0.0)
            image[j, ch, HALO_ROWS:48] = tail8
        if 1 <= j < 9:
            for ch in range(4):
                cots[j - 1, ch, 0:HALO_ROWS] = jnp.where(
                    keep, planes_ref[source, 2 + ch].astype(F32), 0.0
                )
                cots[j - 1, ch, HALO_ROWS:48] = tail8

    def at_edges(rows):
        column = lax.broadcasted_iota(jnp.int32, (rows, NZ), 1)
        return column == 0, column == NZ - 1

    low, high = at_edges(192)
    zero64 = jnp.zeros((64, NZ), BF16)
    for j in range(8):
        a1[j, 960:1024] = zero64
        s1[j, 960:1024] = jnp.zeros((64, NZ), F32)
    for j in range(6):
        a2[j, 960:1024] = zero64
        e2[j, 960:1024] = jnp.zeros((64, 2 * NZ), BF16)
    for j in range(3):
        e1[j, 960:1024] = jnp.zeros((64, 2 * NZ), BF16)

    def first_step(step, carry):
        pair, block = 2 * (step // 5), step % 5
        at = pl.multiple_of(8 * block, 8)
        to = pl.multiple_of(192 * block, 192)
        pieces = []
        for dx in range(3):
            for ch in range(2):
                pieces.append(
                    jnp.concatenate(
                        [
                            image[pair + dx, ch, pl.ds(at, 16)],
                            image[pair + dx + 1, ch, pl.ds(at, 16)],
                        ],
                        1,
                    ).astype(BF16)
                )
        parts = mm(t1_ref[...], jnp.concatenate(pieces, 0))
        for half in range(2):
            pre = join_z(parts, 192, half, low, high)
            gate = jax.nn.sigmoid(pre)
            a1[pair + half, pl.ds(to, 192)] = (pre * gate).astype(BF16)
            s1[pair + half, pl.ds(to, 192)] = gate * (1.0 + pre * (1.0 - gate))
        return carry

    lax.fori_loop(0, 20, first_step, 0, unroll=5)

    def clear(ref, planes, offset, top, bottom, width):
        for j in range(planes):

            @pl.when(jnp.logical_not(inside(slab + offset + j)))
            def _():
                ref[j] = jnp.zeros((1024, width), BF16)

        @pl.when(coil == 0)
        def _():
            for j in range(planes):
                ref[j, 0:top] = jnp.zeros((top, width), BF16)

        @pl.when(coil == 7)
        def _():
            for j in range(planes):
                ref[j, bottom:1024] = jnp.zeros((1024 - bottom, width), BF16)

    clear(a1, 8, -3, 72, 840, NZ)

    def second_step(step, carry):
        pair, block = 2 * (step // 5), step % 5
        at = pl.multiple_of(8 * block, 8)
        to = pl.multiple_of(192 * block, 192)
        stacked = jnp.concatenate(
            [
                jnp.concatenate(
                    [a1[pair + dx, pl.ds(to, 256)], a1[pair + dx + 1, pl.ds(to, 256)]], 1
                )
                for dx in range(3)
            ],
            0,
        )
        parts = mm(t2_ref[...], stacked)
        for half in range(2):
            pre = join_z(parts, 192, half, low, high)
            gate = jax.nn.sigmoid(pre)
            a2[pair + half, pl.ds(to, 192)] = (pre * gate).astype(BF16)
            slope = gate * (1.0 + pre * (1.0 - gate))
            pieces = []
            for dx in range(3):
                for ch in range(2):
                    pieces.append(
                        jnp.concatenate(
                            [
                                cots[pair + half + dx, ch, pl.ds(at, 16)],
                                cots[pair + half + dx, 2 + ch, pl.ds(at, 16)],
                            ],
                            1,
                        ).astype(BF16)
                    )
            back = mm(t3t_ref[...], jnp.concatenate(pieces, 0))
            for which in range(2):
                grad = join_z(back, 192, which, low, high) * slope
                e2[pair + half, pl.ds(to, 192), which * NZ : which * NZ + NZ] = grad.astype(BF16)
        return carry

    lax.fori_loop(0, 15, second_step, 0, unroll=5)
    clear(a2, 6, -2, 48, 816, NZ)
    clear(e2, 6, -2, 48, 816, 2 * NZ)

    def third_step(step, carry):
        plane, block = step // 5, step % 5
        to = pl.multiple_of(192 * block, 192)
        stacked = jnp.concatenate([e2[plane + dx, pl.ds(to, 256)] for dx in range(3)], 0)
        back = mm(t2t_ref[...], stacked)
        slope = s1[plane + 2, pl.ds(to + 48, 192)]
        for which in range(2):
            grad = join_z(back, 192, which, low, high) * slope
            e1[plane, pl.ds(to, 192), which * NZ : which * NZ + NZ] = grad.astype(BF16)
        return carry

    lax.fori_loop(0, 15, third_step, 0, unroll=5)
    clear(e1, 3, -1, 24, 792, 2 * NZ)

    low16, high16 = at_edges(16)
    for pair in range(2):
        stacked = jnp.concatenate(
            [
                jnp.concatenate(
                    [
                        a2[1 + dx, 24 + 384 * pair : 280 + 384 * pair],
                        a2[1 + dx, 216 + 384 * pair : 472 + 384 * pair],
                    ],
                    1,
                )
                for dx in range(3)
            ],
            0,
        )
        parts = mm(t3_ref[...], stacked)
        for half in range(2):
            update = join_z(parts, 16, half, low16, high16)
            at = 16 * pair + 8 * half
            for ch in range(2):
                new_ref[ch, at : at + 8] = (
                    relaxed_ref[ch, at : at + 8] + update[8 * ch : 8 * ch + 8]
                )

    for block in range(4):
        stacked = jnp.concatenate([e1[dx, 192 * block : 192 * block + 256] for dx in range(3)], 0)
        back = mm(t1t_ref[...], stacked)
        for which in range(2):
            grad = join_z(back, 16, which, low16, high16)
            for ch in range(2):
                rows = slice(8 * block, 8 * block + 8)
                if which == 0:
                    base = (2 * bits_ref[ch, rows] - 1).astype(F32)
                else:
                    base = adj_ref[ch, rows]
                pulled_ref[2 * which + ch, rows] = base + grad[8 * ch : 8 * ch + 8]
    for ch in range(4):
        rows = pulled_ref[ch].astype(BF16)
        for dest in range(8):
            send_ref[dest, ch] = rows


def normal_kernel(field_ref, maps_ref, mask_ref, yh, yl, zh, zl, out_ref):
    tabs = (yh, yl, zh, zl)
    weight = mask_ref[...].astype(F32)
    map_re, map_im = maps_ref[0], maps_ref[1]
    for which in range(2):
        re = field_ref[:, 2 * which].reshape(NY, NZ).astype(F32)
        im = field_ref[:, 2 * which + 1].reshape(NY, NZ).astype(F32)
        f_re, f_im = forward(map_re * re - map_im * im, map_re * im + map_im * re, tabs)
        b_re, b_im = inverse(weight * f_re, weight * f_im, tabs)
        out_re = (map_re * b_re + map_im * b_im).astype(BF16)
        out_im = (map_re * b_im - map_im * b_re).astype(BF16)
        for dest in range(8):
            rows = slice(NYL * dest, NYL * dest + NYL)
            out_ref[dest, 2 * which] = out_re[rows]
            out_ref[dest, 2 * which + 1] = out_im[rows]


def final_kernel(got_ref, pulled_ref, loss_ref, probe_ref, next_ref):
    for ch in range(4):
        total = got_ref[0, ch].astype(F32)
        for source in range(1, 8):
            total = total + got_ref[source, ch].astype(F32)
        result = pulled_ref[ch] - STEP * total
        if ch < 2:
            probe_ref[ch] = result
        else:
            next_ref[ch - 2] = loss_ref[ch - 2] + result


def on_device(
    coil_maps,
    kspace,
    sample_mask,
    iterate,
    probe_bits,
    loss_gradient,
    adjoint,
    kernel_first,
    kernel_second,
    kernel_last,
):
    maps = coil_maps[0, :, 0]
    data = kspace[0, :, 0]
    iterate, bits, loss, adj = (
        a[:, 0] for a in (iterate, probe_bits, loss_gradient, adjoint)
    )
    fourier = [jnp.asarray(t) for t in fourier_constants()]
    place = jnp.stack([lax.axis_index("coil"), lax.axis_index("slab")]).astype(jnp.int32)
    smem = pl.BlockSpec(memory_space=pltpu.SMEM)

    toeplitz = tables(kernel_first, kernel_second, kernel_last)
    field = lax.all_to_all(jnp.broadcast_to(iterate[None], (8,) + iterate.shape), "coil", 0, 0)
    partial_sums = pl.pallas_call(
        gradient_kernel,
        out_shape=jax.ShapeDtypeStruct((8, 3, HALO_ROWS, NZ), BF16),
        in_specs=whole(10),
        out_specs=whole(1)[0],
        scratch_shapes=[pltpu.VMEM((2, NY + 8, NZ), F32)],
    )(field, maps, data, sample_mask, bits, adj, *fourier)
    got = lax.all_to_all(partial_sums, "coil", 0, 0)
    payload, relaxed = pl.pallas_call(
        relax_kernel,
        out_shape=[
            jax.ShapeDtypeStruct((16, 6, HALO_ROWS, NZ), BF16),
            jax.ShapeDtypeStruct((2, NYL, NZ), F32),
        ],
        in_specs=[smem] + whole(4),
        out_specs=whole(2),
        scratch_shapes=[pltpu.VMEM((2, NY + 8, NZ), F32), pltpu.VMEM((4, HALO_ROWS, NZ), F32)],
    )(place, got, field, bits, adj)
    planes = lax.all_to_all(payload, "slab", 0, 0)
    new_iterate, pulled, send = pl.pallas_call(
        denoise_kernel,
        out_shape=[
            jax.ShapeDtypeStruct((2, NYL, NZ), F32),
            jax.ShapeDtypeStruct((4, NYL, NZ), F32),
            jax.ShapeDtypeStruct((8, 4, NYL, NZ), BF16),
        ],
        in_specs=[smem] + whole(10),
        out_specs=whole(3),
        scratch_shapes=[
            pltpu.VMEM((10, 2, 48, NZ), F32),
            pltpu.VMEM((8, 4, 48, NZ), F32),
            pltpu.VMEM((8, 1024, NZ), BF16),
            pltpu.VMEM((8, 1024, NZ), F32),
            pltpu.VMEM((6, 1024, NZ), BF16),
            pltpu.VMEM((6, 1024, 2 * NZ), BF16),
            pltpu.VMEM((3, 1024, 2 * NZ), BF16),
        ],
        compiler_params=pltpu.CompilerParams(vmem_limit_bytes=VMEM_BIG),
    )(place, planes, relaxed, bits, adj, *toeplitz)
    spread = lax.all_to_all(send, "coil", 0, 0)
    back = pl.pallas_call(
        normal_kernel,
        out_shape=jax.ShapeDtypeStruct((8, 4, NYL, NZ), BF16),
        in_specs=whole(7),
        out_specs=whole(1)[0],
    )(spread, maps, sample_mask, *fourier)
    back = lax.all_to_all(back, "coil", 0, 0)
    probe, following = pl.pallas_call(
        final_kernel,
        out_shape=[jax.ShapeDtypeStruct((2, NYL, NZ), F32)] * 2,
        in_specs=whole(3),
        out_specs=whole(2),
    )(back, pulled, loss)
    return new_iterate[:, None], probe[:, None], following[:, None]


def solution(mesh):
    image = P(None, "slab", "coil", None)
    coils = P("coil", None, "slab", None, None)
    return jax.shard_map(
        on_device,
        mesh=mesh,
        in_specs=(coils, coils, P(), image, image, image, image, P(), P(), P()),
        out_specs=(image, image, image),
        check_vma=False,
    )
```

```python
import math

import jax
import jax.numpy as jnp
import numpy as np
from jax import lax
from jax.experimental import pallas as pl
from jax.experimental.pallas import tpu as pltpu
from jax.sharding import PartitionSpec as P

STEP = 0.8
F32 = jnp.float32
BF16 = jnp.bfloat16
NZ = 128
NY = 256
NYL = 32
HALO_ROWS = 40
HALF = 16
PART_ROWS = 24
GRANT = pltpu.CompilerParams(vmem_limit_bytes=24 << 20)


def whole(count):
    return [pl.BlockSpec(memory_space=pltpu.VMEM)] * count


def split_host(table):
    high = table.astype(np.float32).astype(jnp.bfloat16)
    low = (table - high.astype(np.float64)).astype(jnp.bfloat16)
    return high, low


def fourier_constants():
    def cos_sin(length):
        index = np.arange(length)
        angles = (index[:, None] * index[None, :] % length) * (2.0 * math.pi / length)
        return np.cos(angles) / math.sqrt(length), np.sin(angles) / math.sqrt(length)

    cos_y, sin_y = cos_sin(NY)
    cos_z, sin_z = cos_sin(NZ)
    along_y = np.concatenate([cos_y, sin_y], axis=0)
    along_z = np.block([[cos_z, -sin_z], [sin_z, cos_z]])
    return split_host(along_y) + split_host(along_z)


def split(values):
    high = values.astype(BF16)
    return high, (values - high.astype(F32)).astype(BF16)


def mm(left, right):
    return jnp.dot(left, right, preferred_element_type=F32)


def along_z(joined, high_ref, low_ref):
    high, low = split(joined)
    return mm(high, high_ref[...]) + (mm(high, low_ref[...]) + mm(low, high_ref[...]))


def along_y(joined, high_ref, low_ref):
    high, low = split(joined)
    return mm(high_ref[...], high) + (mm(low_ref[...], high) + mm(high_ref[...], low))


def forward(real, imag, tabs):
    y_high, y_low, z_high, z_low = tabs
    turned = along_y(along_z(jnp.concatenate([real, imag], 1), z_high, z_low), y_high, y_low)
    cos_part, sin_part = turned[:NY], turned[NY:]
    return cos_part[:, :NZ] + sin_part[:, NZ:], cos_part[:, NZ:] - sin_part[:, :NZ]


def inverse(real, imag, tabs):
    y_high, y_low, z_high, z_low = tabs
    turned = along_y(jnp.concatenate([real, imag], 1), y_high, y_low)
    cos_part, sin_part = turned[:NY], turned[NY:]
    back = cos_part[:, :NZ] - sin_part[:, NZ:], -(cos_part[:, NZ:] + sin_part[:, :NZ])
    turned = along_z(jnp.concatenate(back, 1), z_high, z_low)
    return turned[:, :NZ], -turned[:, NZ:]


def gradient_kernel(
    field_ref,
    maps_ref,
    kspace_ref,
    mask_ref,
    iterate_ref,
    bits_ref,
    adj_ref,
    yh,
    yl,
    zh,
    zl,
    out_ref,
    pad,
):
    tabs = (yh, yl, zh, zl)
    weight = mask_ref[...].astype(F32)
    map_re, map_im = maps_ref[0], maps_ref[1]
    re = field_ref[:, 0].astype(F32).reshape(NY, NZ)
    im = field_ref[:, 1].astype(F32).reshape(NY, NZ)
    f_re, f_im = forward(map_re * re - map_im * im, map_re * im + map_im * re, tabs)
    f_re = weight * (f_re - kspace_ref[0])
    f_im = weight * (f_im - kspace_ref[1])
    b_re, b_im = inverse(f_re, f_im, tabs)
    zero = jnp.zeros((4, NZ), F32)
    for ch in range(2):
        pad[ch, 0:4] = zero
        pad[ch, NY + 4 : NY + 8] = zero
    pad[0, 4 : NY + 4] = map_re * b_re + map_im * b_im
    pad[1, 4 : NY + 4] = map_re * b_im - map_im * b_re
    edges = []
    for ch in range(6):
        if ch < 2:
            rows = (2 * bits_ref[ch] - 1).astype(F32)
        elif ch < 4:
            rows = adj_ref[ch - 2]
        else:
            rows = split(iterate_ref[ch - 4])[1].astype(F32)
        edges += [rows[0:4], rows[NYL - 4 : NYL]]
    edges = jnp.concatenate(edges, 0).astype(BF16)
    for dest in range(8):
        for ch in range(2):
            out_ref[dest, HALO_ROWS * ch : HALO_ROWS * ch + HALO_ROWS] = pad[
                ch, NYL * dest : NYL * dest + HALO_ROWS
            ].astype(BF16)
        out_ref[dest, 80:128] = edges


def relax_kernel(
    got_ref, field_ref, iterate_ref, bits_ref, adj_ref, out_ref, relaxed_ref, pad, qpad
):
    coil = lax.axis_index("coil")
    lower, upper = jnp.maximum(coil - 1, 0), jnp.minimum(coil + 1, 7)
    below = jnp.where(coil > 0, got_ref[lower, 80:128].astype(F32), 0.0)
    above = jnp.where(coil < 7, got_ref[upper, 80:128].astype(F32), 0.0)
    for ch in range(2):
        under = jnp.where(coil > 0, field_ref[lower, ch].astype(F32), 0.0)
        over = jnp.where(coil < 7, field_ref[upper, ch].astype(F32), 0.0)
        at = 32 + 8 * ch
        pad[ch, 0:4] = under[NYL - 4 : NYL] + below[at + 4 : at + 8]
        pad[ch, 4 : 4 + NYL] = iterate_ref[ch]
        pad[ch, 4 + NYL : HALO_ROWS] = over[0:4] + above[at : at + 4]
        rows = slice(HALO_ROWS * ch, HALO_ROWS * ch + HALO_ROWS)
        total = got_ref[0, rows].astype(F32)
        for source in range(1, 8):
            total = total + got_ref[source, rows].astype(F32)
        relaxed = pad[ch] - STEP * total
        relaxed_ref[ch] = relaxed[4 : 4 + NYL]
        rows = relaxed.astype(BF16)
        for dest in range(16):
            first = HALF * (dest % 2)
            out_ref[dest, ch] = rows[first : first + PART_ROWS]
    for ch in range(4):
        if ch < 2:
            rows = (2 * bits_ref[ch] - 1).astype(F32)
        else:
            rows = adj_ref[ch - 2]
        qpad[ch, 0:3] = below[ch * 8 + 5 : ch * 8 + 8]
        qpad[ch, 3 : 3 + NYL] = rows
        qpad[ch, 3 + NYL : 7 + NYL] = above[ch * 8 : ch * 8 + 4]
        qpad[ch, 7 + NYL : HALO_ROWS] = jnp.zeros((1, NZ), F32)
        rows = qpad[ch].astype(BF16)
        for dest in range(16):
            first = HALF * (dest % 2)
            out_ref[dest, 2 + ch] = rows[first : first + PART_ROWS]


def dot_first(left, right):
    return lax.dot_general(left, right, (((0,), (0,)), ((), ())), preferred_element_type=F32)


def tables_kernel(k1_ref, k2_ref, k3_ref, t1_ref, t2_ref, t3_ref, t1t_ref, t2t_ref, t3t_ref):
    lane = lax.broadcasted_iota(jnp.int32, (24, 256), 1)
    row = lax.broadcasted_iota(jnp.int32, (24, 256), 0)
    tile24 = ((lane % 24 == row) & (lane < 240)).astype(BF16)
    window = jnp.where(lane < 240, lane // 24, 99)

    def tap(dx, dy, dz, flip):
        if flip:
            dx, dy, dz = 2 - dx, 2 - dy, 2 - dz
        return dx * 9 + dy * 3 + dz

    for target, flip in ((t2_ref, False), (t2t_ref, True)):
        for dz in range(3):
            for dx in range(3):
                spread = []
                for dy in range(3):
                    block = k2_ref[tap(dx, dy, dz, flip)]
                    spread.append(dot_first(block, tile24) if flip else mm(block, tile24))
                for yo in range(8):
                    value = jnp.zeros((24, 256), F32)
                    for dy in range(3):
                        value = jnp.where(window == yo + dy, spread[dy], value)
                    at = dz * 192 + yo * 24
                    target[at : at + 24, dx * 256 : dx * 256 + 256] = value.astype(BF16)

    lane96 = lax.broadcasted_iota(jnp.int32, (24, 96), 1)
    lane2 = lax.broadcasted_iota(jnp.int32, (2, 96), 1)
    row2 = lax.broadcasted_iota(jnp.int32, (2, 96), 0)
    tile2 = ((lane2 // 16) % 2 == row2).astype(BF16)
    code = (lane96 // 32) * 16 + lane96 % 16
    for target, source, flip in ((t1_ref, k1_ref, False), (t3t_ref, k3_ref, True)):
        for dz in range(3):
            spread = {}
            for dx in range(3):
                for dy in range(3):
                    spread[dx, dy] = dot_first(source[tap(dx, dy, dz, flip)], tile2)
            for yo in range(8):
                value = jnp.zeros((24, 96), F32)
                for dx in range(3):
                    for dy in range(3):
                        value = jnp.where(code == dx * 16 + yo + dy, spread[dx, dy], value)
                at = dz * 192 + yo * 24
                target[at : at + 24, :] = value.astype(BF16)

    window8 = window[0:8] - lax.broadcasted_iota(jnp.int32, (8, 256), 0)
    for target, source, flip in ((t3_ref, k3_ref, False), (t1t_ref, k1_ref, True)):
        for dz in range(3):
            for dx in range(3):
                spread = [mm(source[tap(dx, dy, dz, flip)], tile24) for dy in range(3)]
                both = []
                for ch in range(2):
                    value = jnp.zeros((8, 256), F32)
                    for dy in range(3):
                        value = jnp.where(window8 == dy, spread[dy][ch : ch + 1], value)
                    both.append(value)
                target[dz * 16 : dz * 16 + 16, dx * 256 : dx * 256 + 256] = jnp.concatenate(
                    both, 0
                ).astype(BF16)


def tables(kernel_first, kernel_second, kernel_last):
    k1 = jnp.transpose(kernel_first, (2, 3, 4, 1, 0)).reshape(27, 2, 24)
    k2 = jnp.transpose(kernel_second, (2, 3, 4, 0, 1)).reshape(27, 24, 24)
    k3 = jnp.transpose(kernel_last, (2, 3, 4, 0, 1)).reshape(27, 2, 24)
    shapes = [(576, 96), (576, 768), (48, 768), (48, 768), (576, 768), (576, 96)]
    return pl.pallas_call(
        tables_kernel,
        compiler_params=GRANT,
        out_shape=[jax.ShapeDtypeStruct(s, BF16) for s in shapes],
        in_specs=whole(3),
        out_specs=whole(6),
        cost_estimate=pl.CostEstimate(flops=10**9, bytes_accessed=4 * 10**6, transcendentals=0),
    )(k1, k2, k3)


def join_z(parts, rows, half, at_low, at_high):
    lanes = slice(half * NZ, half * NZ + NZ)
    before = jnp.where(at_low, 0.0, pltpu.roll(parts[0:rows, lanes], 1, 1))
    after = jnp.where(at_high, 0.0, pltpu.roll(parts[2 * rows : 3 * rows, lanes], NZ - 1, 1))
    return parts[rows : 2 * rows, lanes] + (before + after)


def denoise_kernel(
    planes_ref,
    t1_ref,
    t2_ref,
    t3_ref,
    t1t_ref,
    t2t_ref,
    t3t_ref,
    send_ref,
    pair_ref,
    image,
    cots,
    a1,
    s1,
    a2,
    e2,
    e1,
):
    coil, slab = lax.axis_index("coil"), lax.axis_index("slab")
    base, side = 2 * (slab // 2), slab % 2

    def inside(plane):
        return (plane >= 0) & (plane < 16)

    for j in range(10):
        plane = base - 4 + j
        keep = inside(plane)
        source = jnp.clip(plane, 0, 15)
        for ch in range(2):
            image[j, ch, 0:PART_ROWS] = jnp.where(keep, planes_ref[source, ch].astype(F32), 0.0)
            image[j, ch, PART_ROWS:32] = jnp.zeros((8, NZ), F32)
        if 1 <= j < 9:
            for ch in range(4):
                cots[j - 1, ch, 0:PART_ROWS] = jnp.where(
                    keep, planes_ref[source, 2 + ch].astype(F32), 0.0
                )
                cots[j - 1, ch, PART_ROWS:32] = jnp.zeros((8, NZ), F32)

    def at_edges(rows):
        column = lax.broadcasted_iota(jnp.int32, (rows, NZ), 1)
        return column == 0, column == NZ - 1

    for j in range(8):
        a1[j, 576:640] = jnp.zeros((64, NZ), BF16)
        s1[j, 576:640] = jnp.zeros((64, NZ), F32)
    for j in range(6):
        e2[j, 480:640] = jnp.zeros((160, 2 * NZ), BF16)

    def rows_of(table_ref, rows):
        if rows == 192:
            return table_ref[...]
        return jnp.concatenate([table_ref[192 * dz : 192 * dz + rows] for dz in range(3)], 0)

    def first_step(step, carry):
        pair, block = 2 * (step // 3), step % 3
        at = pl.multiple_of(8 * block, 8)
        to = pl.multiple_of(192 * block, 192)
        pieces = []
        for dx in range(3):
            for ch in range(2):
                pieces.append(
                    jnp.concatenate(
                        [
                            image[pair + dx, ch, pl.ds(at, 16)],
                            image[pair + dx + 1, ch, pl.ds(at, 16)],
                        ],
                        1,
                    ).astype(BF16)
                )
        parts = mm(t1_ref[...], jnp.concatenate(pieces, 0))
        low, high = at_edges(192)
        for half in range(2):
            pre = join_z(parts, 192, half, low, high)
            gate = jax.nn.sigmoid(pre)
            a1[pair + half, pl.ds(to, 192)] = (pre * gate).astype(BF16)
            s1[pair + half, pl.ds(to, 192)] = gate * (1.0 + pre * (1.0 - gate))
        return carry

    lax.fori_loop(0, 12, first_step, 0, unroll=6)

    def clear(ref, planes, offset, top, bottom):
        rows, width = ref.shape[1], ref.shape[2]
        for j in range(planes):

            @pl.when(jnp.logical_not(inside(base + offset + j)))
            def _():
                ref[j] = jnp.zeros((rows, width), BF16)

        @pl.when((coil == 0) & (side == 0))
        def _():
            for j in range(planes):
                ref[j, 0:top] = jnp.zeros((top, width), BF16)

        @pl.when((coil == 7) & (side == 1))
        def _():
            for j in range(planes):
                ref[j, bottom:rows] = jnp.zeros((rows - bottom, width), BF16)

    clear(a1, 8, -3, 72, 456)

    def second_block(pair, at, to, rows):
        stacked = jnp.concatenate(
            [
                jnp.concatenate(
                    [a1[pair + dx, pl.ds(to, 256)], a1[pair + dx + 1, pl.ds(to, 256)]], 1
                )
                for dx in range(3)
            ],
            0,
        )
        parts = mm(rows_of(t2_ref, rows), stacked)
        low, high = at_edges(rows)
        for half in range(2):
            pre = join_z(parts, rows, half, low, high)
            gate = jax.nn.sigmoid(pre)
            a2[pair + half, pl.ds(to, rows)] = (pre * gate).astype(BF16)
            slope = gate * (1.0 + pre * (1.0 - gate))
            pieces = []
            for dx in range(3):
                for ch in range(2):
                    pieces.append(
                        jnp.concatenate(
                            [
                                cots[pair + half + dx, ch, pl.ds(at, 16)],
                                cots[pair + half + dx, 2 + ch, pl.ds(at, 16)],
                            ],
                            1,
                        ).astype(BF16)
                    )
            back = mm(rows_of(t3t_ref, rows), jnp.concatenate(pieces, 0))
            for which in range(2):
                grad = join_z(back, rows, which, low, high) * slope
                e2[pair + half, pl.ds(to, rows), which * NZ : which * NZ + NZ] = grad.astype(BF16)

    def second_step(step, carry):
        pair = 2 * step
        second_block(pair, 0, 0, 192)
        second_block(pair, 8, 192, 192)
        second_block(pair, 16, 384, 96)
        return carry

    lax.fori_loop(0, 3, second_step, 0)
    clear(a2, 6, -2, 48, 432)
    clear(e2, 6, -2, 48, 432)

    def third_block(plane, to, rows):
        stacked = jnp.concatenate([e2[plane + dx, pl.ds(to, 256)] for dx in range(3)], 0)
        back = mm(rows_of(t2t_ref, rows), stacked)
        low, high = at_edges(rows)
        slope = s1[plane + 2, pl.ds(to + 48, rows)]
        for which in range(2):
            grad = join_z(back, rows, which, low, high) * slope
            e1[plane, pl.ds(to, rows), which * NZ : which * NZ + NZ] = grad.astype(BF16)

    def third_step(step, carry):
        for plane in (2 * step, 2 * step + 1):
            third_block(plane, 0, 192)
            third_block(plane, 192, 192)
            third_block(plane, 384, 48)
        return carry

    lax.fori_loop(0, 2, third_step, 0)
    for j in range(4):
        e1[j, 432:448] = jnp.zeros((16, 2 * NZ), BF16)
    clear(e1, 4, -1, 24, 408)

    low, high = at_edges(16)
    for block in range(2):
        rows = slice(8 * block, 8 * block + 8)
        window = slice(24 + 192 * block, 280 + 192 * block)
        stacked = jnp.concatenate(
            [jnp.concatenate([a2[1 + dx, window], a2[2 + dx, window]], 1) for dx in range(3)], 0
        )
        parts = mm(t3_ref[...], stacked)
        for p in range(2):
            update = join_z(parts, 16, p, low, high)
            for ch in range(2):
                pair_ref[p, 4 + ch, rows] = update[8 * ch : 8 * ch + 8]

    for p in range(2):
        for block in range(2):
            rows = slice(8 * block, 8 * block + 8)
            shifted = slice(3 + 8 * block, 11 + 8 * block)
            window = slice(192 * block, 192 * block + 256)
            stacked = jnp.concatenate([e1[p + dx, window] for dx in range(3)], 0)
            back = mm(t1t_ref[...], stacked)
            for which in range(2):
                grad = join_z(back, 16, which, low, high)
                for ch in range(2):
                    pair_ref[p, 2 * which + ch, rows] = grad[8 * ch : 8 * ch + 8]
        for ch in range(4):
            pulled = cots[3 + p, ch, 3 : 3 + HALF] + pair_ref[p, ch]
            pulled = pulled.astype(BF16)
            for dest in range(8):
                send_ref[2 * dest + p, ch] = pulled


def normal_kernel(field_ref, maps_ref, mask_ref, yh, yl, zh, zl, out_ref):
    tabs = (yh, yl, zh, zl)
    weight = mask_ref[...].astype(F32)
    map_re, map_im = maps_ref[0], maps_ref[1]
    for which in range(2):
        re = field_ref[:, 2 * which].reshape(NY, NZ).astype(F32)
        im = field_ref[:, 2 * which + 1].reshape(NY, NZ).astype(F32)
        f_re, f_im = forward(map_re * re - map_im * im, map_re * im + map_im * re, tabs)
        b_re, b_im = inverse(weight * f_re, weight * f_im, tabs)
        out_re = (map_re * b_re + map_im * b_im).astype(BF16)
        out_im = (map_re * b_im - map_im * b_re).astype(BF16)
        for dest in range(8):
            rows = slice(NYL * dest, NYL * dest + NYL)
            out_ref[dest, 2 * which] = out_re[rows]
            out_ref[dest, 2 * which + 1] = out_im[rows]


def final_kernel(
    got_ref, pair_ref, relaxed_ref, bits_ref, adj_ref, loss_ref, new_ref, probe_ref, next_ref
):
    for ch in range(2):
        for side in range(2):
            rows = slice(HALF * side, HALF * side + HALF)
            new_ref[ch, rows] = relaxed_ref[ch, rows] + pair_ref[side, 4 + ch]
    for ch in range(4):
        total = got_ref[0, ch].astype(F32)
        for source in range(1, 8):
            total = total + got_ref[source, ch].astype(F32)
        total = STEP * total
        for side in range(2):
            rows = slice(HALF * side, HALF * side + HALF)
            if ch < 2:
                base = (2 * bits_ref[ch, rows] - 1).astype(F32)
                probe_ref[ch, rows] = base + pair_ref[side, ch] - total[rows]
            else:
                base = adj_ref[ch - 2, rows]
                result = base + pair_ref[side, ch] - total[rows]
                next_ref[ch - 2, rows] = loss_ref[ch - 2, rows] + result


def on_device(
    coil_maps,
    kspace,
    sample_mask,
    iterate,
    probe_bits,
    loss_gradient,
    adjoint,
    kernel_first,
    kernel_second,
    kernel_last,
):
    maps = coil_maps[0, :, 0]
    data = kspace[0, :, 0]
    iterate, bits, loss, adj = (a[:, 0] for a in (iterate, probe_bits, loss_gradient, adjoint))
    fourier = [jnp.asarray(t) for t in fourier_constants()]
    slabs = lax.axis_size("slab")
    coils = lax.axis_size("coil")
    twins = [[2 * j, 2 * j + 1] for j in range(slabs // 2)]
    families = [
        [c * slabs + 2 * j + h for c in range(coils) for h in range(2)] for j in range(slabs // 2)
    ]

    toeplitz = tables(kernel_first, kernel_second, kernel_last)
    field = lax.all_to_all(
        jnp.broadcast_to(iterate.astype(BF16)[None], (coils,) + iterate.shape), "coil", 0, 0
    )
    partial_sums = pl.pallas_call(
        gradient_kernel,
        compiler_params=GRANT,
        out_shape=jax.ShapeDtypeStruct((8, 128, NZ), BF16),
        in_specs=whole(11),
        out_specs=whole(1)[0],
        scratch_shapes=[pltpu.VMEM((2, NY + 8, NZ), F32)],
    )(field, maps, data, sample_mask, iterate, bits, adj, *fourier)
    got = lax.all_to_all(partial_sums, "coil", 0, 0)
    payload, relaxed = pl.pallas_call(
        relax_kernel,
        compiler_params=GRANT,
        out_shape=[
            jax.ShapeDtypeStruct((16, 6, PART_ROWS, NZ), BF16),
            jax.ShapeDtypeStruct((2, NYL, NZ), F32),
        ],
        in_specs=whole(5),
        out_specs=whole(2),
        scratch_shapes=[
            pltpu.VMEM((2, HALO_ROWS, NZ), F32),
            pltpu.VMEM((4, HALO_ROWS, NZ), F32),
        ],
    )(got, field, iterate, bits, adj)
    planes = lax.all_to_all(payload, "slab", 0, 0)
    send, pair = pl.pallas_call(
        denoise_kernel,
        compiler_params=GRANT,
        out_shape=[
            jax.ShapeDtypeStruct((16, 4, HALF, NZ), BF16),
            jax.ShapeDtypeStruct((2, 6, HALF, NZ), F32),
        ],
        in_specs=whole(7),
        out_specs=whole(2),
        scratch_shapes=[
            pltpu.VMEM((10, 2, 32, NZ), F32),
            pltpu.VMEM((8, 4, 32, NZ), F32),
            pltpu.VMEM((8, 640, NZ), BF16),
            pltpu.VMEM((8, 640, NZ), F32),
            pltpu.VMEM((6, 480, NZ), BF16),
            pltpu.VMEM((6, 640, 2 * NZ), BF16),
            pltpu.VMEM((4, 448, 2 * NZ), BF16),
        ],
    )(planes, *toeplitz)
    spread = lax.all_to_all(send, ("coil", "slab"), 0, 0, axis_index_groups=families)
    pair = lax.all_to_all(pair, "slab", 0, 0, axis_index_groups=twins)
    back = pl.pallas_call(
        normal_kernel,
        compiler_params=GRANT,
        out_shape=jax.ShapeDtypeStruct((8, 4, NYL, NZ), BF16),
        in_specs=whole(7),
        out_specs=whole(1)[0],
    )(spread, maps, sample_mask, *fourier)
    back = lax.all_to_all(back, "coil", 0, 0)
    new_iterate, probe, following = pl.pallas_call(
        final_kernel,
        compiler_params=GRANT,
        out_shape=[jax.ShapeDtypeStruct((2, NYL, NZ), F32)] * 3,
        in_specs=whole(6),
        out_specs=whole(3),
    )(back, pair, relaxed, bits, adj, loss)
    return new_iterate[:, None], probe[:, None], following[:, None]


def solution(mesh):
    image = P(None, "slab", "coil", None)
    coils = P("coil", None, "slab", None, None)
    return jax.shard_map(
        on_device,
        mesh=mesh,
        in_specs=(coils, coils, P(), image, image, image, image, P(), P(), P()),
        out_specs=(image, image, image),
        check_vma=False,
    )
```

```python
import math

import jax
import jax.numpy as jnp
import numpy as np
from jax import lax
from jax.experimental import pallas as pl
from jax.experimental.pallas import tpu as pltpu
from jax.sharding import PartitionSpec as P

STEP = 0.8
F32 = jnp.float32
BF16 = jnp.bfloat16
NZ = 128
NY = 256
NYL = 32
HALO_ROWS = 40
HALF = 16
PART_ROWS = 24
GRANT = pltpu.CompilerParams(vmem_limit_bytes=24 << 20)


def whole(count):
    return [pl.BlockSpec(memory_space=pltpu.VMEM)] * count


def split_host(table):
    high = table.astype(np.float32).astype(jnp.bfloat16)
    low = (table - high.astype(np.float64)).astype(jnp.bfloat16)
    return high, low


def fourier_constants():
    def cos_sin(length):
        index = np.arange(length)
        angles = (index[:, None] * index[None, :] % length) * (2.0 * math.pi / length)
        return np.cos(angles) / math.sqrt(length), np.sin(angles) / math.sqrt(length)

    cos_y, sin_y = cos_sin(NY)
    cos_z, sin_z = cos_sin(NZ)
    along_y = np.concatenate([cos_y, sin_y], axis=0)
    along_z = np.block([[cos_z, -sin_z], [sin_z, cos_z]])
    return jnp.asarray(np.concatenate(split_host(along_y) + split_host(along_z), axis=0))


def split(values):
    high = values.astype(BF16)
    return high, (values - high.astype(F32)).astype(BF16)


def mm(left, right):
    return jnp.dot(left, right, preferred_element_type=F32)


def along_z(joined, tab_ref):
    high, low = split(joined)
    z_high, z_low = tab_ref[1024:1280], tab_ref[1280:1536]
    return mm(high, z_high) + (mm(high, z_low) + mm(low, z_high))


def along_y(joined, tab_ref):
    high, low = split(joined)
    y_high, y_low = tab_ref[0:512], tab_ref[512:1024]
    return mm(y_high, high) + (mm(y_low, high) + mm(y_high, low))


def forward(real, imag, tab_ref):
    turned = along_y(along_z(jnp.concatenate([real, imag], 1), tab_ref), tab_ref)
    cos_part, sin_part = turned[:NY], turned[NY:]
    return cos_part[:, :NZ] + sin_part[:, NZ:], cos_part[:, NZ:] - sin_part[:, :NZ]


def inverse(real, imag, tab_ref):
    turned = along_y(jnp.concatenate([real, imag], 1), tab_ref)
    cos_part, sin_part = turned[:NY], turned[NY:]
    back = cos_part[:, :NZ] - sin_part[:, NZ:], -(cos_part[:, NZ:] + sin_part[:, :NZ])
    turned = along_z(jnp.concatenate(back, 1), tab_ref)
    return turned[:, :NZ], -turned[:, NZ:]


def stage_kernel(
    maps_in,
    kspace_in,
    mask_in,
    iterate_in,
    bits_in,
    adj_in,
    tab_in,
    k1_in,
    k2_in,
    k3_in,
    maps_ref,
    masked_ref,
    weight_ref,
    own_ref,
    edges_ref,
    tab_ref,
    first_ref,
    all_ref,
    mask_ref,
    bits_ref,
    k1_ref,
    k2_ref,
    k3_ref,
    sems,
):
    moves = (
        (k1_in, k1_ref),
        (k2_in, k2_ref),
        (k3_in, k3_ref),
        (iterate_in, own_ref.at[0:2]),
        (bits_in, bits_ref),
        (adj_in, own_ref.at[4:6]),
        (mask_in, mask_ref),
        (kspace_in, masked_ref),
        (maps_in, maps_ref),
        (tab_in, tab_ref),
    )
    copies = [pltpu.make_async_copy(s, d, sems.at[i]) for i, (s, d) in enumerate(moves)]
    for copy in copies:
        copy.start()
    for copy in copies[0:3]:
        copy.wait()
    build_tables(k1_ref, k2_ref, k3_ref, all_ref)
    for copy in copies[3:]:
        copy.wait()
    for ch in range(2):
        rows = own_ref[ch].astype(BF16)
        for dest in range(8):
            first_ref[dest, ch] = rows
    weight = mask_ref[...].astype(F32)
    weight_ref[...] = weight
    for ch in range(2):
        masked_ref[ch] = weight * masked_ref[ch]
        own_ref[2 + ch] = (2 * bits_ref[ch] - 1).astype(F32)
    edges = []
    for ch in (2, 3, 4, 5, 0, 1):
        rows = own_ref[ch]
        if ch < 2:
            rows = split(rows)[1].astype(F32)
        edges += [rows[0:4], rows[NYL - 4 : NYL]]
    edges_ref[...] = jnp.concatenate(edges, 0).astype(BF16)


def gradient_kernel(
    field_ref, maps_ref, masked_ref, weight_ref, edges_ref, tab_ref, out_ref, pad
):
    weight = weight_ref[...]
    map_re, map_im = maps_ref[0], maps_ref[1]
    re = field_ref[:, 0].astype(F32).reshape(NY, NZ)
    im = field_ref[:, 1].astype(F32).reshape(NY, NZ)
    f_re, f_im = forward(map_re * re - map_im * im, map_re * im + map_im * re, tab_ref)
    f_re = weight * f_re - masked_ref[0]
    f_im = weight * f_im - masked_ref[1]
    b_re, b_im = inverse(f_re, f_im, tab_ref)
    zero = jnp.zeros((4, NZ), F32)
    for ch in range(2):
        pad[ch, 0:4] = zero
        pad[ch, NY + 4 : NY + 8] = zero
    pad[0, 4 : NY + 4] = map_re * b_re + map_im * b_im
    pad[1, 4 : NY + 4] = map_re * b_im - map_im * b_re
    edges = edges_ref[...]
    for dest in range(8):
        for ch in range(2):
            out_ref[dest, HALO_ROWS * ch : HALO_ROWS * ch + HALO_ROWS] = pad[
                ch, NYL * dest : NYL * dest + HALO_ROWS
            ].astype(BF16)
        out_ref[dest, 80:128] = edges


def relax_kernel(got_ref, field_ref, own_ref, out_ref, relaxed_ref, pad, qpad):
    coil = lax.axis_index("coil")
    lower, upper = jnp.maximum(coil - 1, 0), jnp.minimum(coil + 1, 7)
    below = jnp.where(coil > 0, got_ref[lower, 80:128].astype(F32), 0.0)
    above = jnp.where(coil < 7, got_ref[upper, 80:128].astype(F32), 0.0)
    for ch in range(2):
        under = jnp.where(coil > 0, field_ref[lower, ch].astype(F32), 0.0)
        over = jnp.where(coil < 7, field_ref[upper, ch].astype(F32), 0.0)
        at = 32 + 8 * ch
        pad[ch, 0:4] = under[NYL - 4 : NYL] + below[at + 4 : at + 8]
        pad[ch, 4 : 4 + NYL] = own_ref[ch]
        pad[ch, 4 + NYL : HALO_ROWS] = over[0:4] + above[at : at + 4]
        rows = slice(HALO_ROWS * ch, HALO_ROWS * ch + HALO_ROWS)
        total = got_ref[0, rows].astype(F32)
        for source in range(1, 8):
            total = total + got_ref[source, rows].astype(F32)
        relaxed = pad[ch] - STEP * total
        relaxed_ref[ch] = relaxed[4 : 4 + NYL]
        rows = relaxed.astype(BF16)
        for dest in range(16):
            first = HALF * (dest % 2)
            out_ref[dest, ch] = rows[first : first + PART_ROWS]
    for ch in range(4):
        qpad[ch, 0:3] = below[ch * 8 + 5 : ch * 8 + 8]
        qpad[ch, 3 : 3 + NYL] = own_ref[2 + ch]
        qpad[ch, 3 + NYL : 7 + NYL] = above[ch * 8 : ch * 8 + 4]
        qpad[ch, 7 + NYL : HALO_ROWS] = jnp.zeros((1, NZ), F32)
        rows = qpad[ch].astype(BF16)
        for dest in range(16):
            first = HALF * (dest % 2)
            out_ref[dest, 2 + ch] = rows[first : first + PART_ROWS]


def dot_first(left, right):
    return lax.dot_general(left, right, (((0,), (0,)), ((), ())), preferred_element_type=F32)


def build_tables(k1_ref, k2_ref, k3_ref, all_ref):
    t2_ref, t2t_ref = all_ref.at[0:576, 0:768], all_ref.at[576:1152, 0:768]
    t1_ref, t3t_ref = all_ref.at[0:576, 768:896], all_ref.at[576:1152, 768:896]
    t3_ref, t1t_ref = all_ref.at[1152:1200, 0:768], all_ref.at[1200:1248, 0:768]
    lane = lax.broadcasted_iota(jnp.int32, (24, 256), 1)
    row = lax.broadcasted_iota(jnp.int32, (24, 256), 0)
    tile24 = ((lane % 24 == row) & (lane < 240)).astype(BF16)
    window = jnp.where(lane < 240, lane // 24, 99)

    def tap(dx, dy, dz, flip):
        if flip:
            dx, dy, dz = 2 - dx, 2 - dy, 2 - dz
        return dx * 9 + dy * 3 + dz

    for target, flip in ((t2_ref, False), (t2t_ref, True)):
        for dz in range(3):
            for dx in range(3):
                spread = []
                for dy in range(3):
                    block = k2_ref[tap(dx, dy, dz, flip)]
                    spread.append(dot_first(block, tile24) if flip else mm(block, tile24))
                for yo in range(8):
                    value = jnp.zeros((24, 256), F32)
                    for dy in range(3):
                        value = jnp.where(window == yo + dy, spread[dy], value)
                    at = dz * 192 + yo * 24
                    target[at : at + 24, dx * 256 : dx * 256 + 256] = value.astype(BF16)

    lane96 = lax.broadcasted_iota(jnp.int32, (24, 128), 1)
    lane2 = lax.broadcasted_iota(jnp.int32, (2, 128), 1)
    row2 = lax.broadcasted_iota(jnp.int32, (2, 128), 0)
    tile2 = ((lane2 // 16) % 2 == row2).astype(BF16)
    code = (lane96 // 32) * 16 + lane96 % 16
    for target, source, flip in ((t1_ref, k1_ref, False), (t3t_ref, k3_ref, True)):
        for dz in range(3):
            spread = {}
            for dx in range(3):
                for dy in range(3):
                    spread[dx, dy] = dot_first(source[tap(dx, dy, dz, flip)], tile2)
            for yo in range(8):
                value = jnp.zeros((24, 128), F32)
                for dx in range(3):
                    for dy in range(3):
                        value = jnp.where(code == dx * 16 + yo + dy, spread[dx, dy], value)
                at = dz * 192 + yo * 24
                target[at : at + 24, :] = value.astype(BF16)

    window8 = window[0:8] - lax.broadcasted_iota(jnp.int32, (8, 256), 0)
    for target, source, flip in ((t3_ref, k3_ref, False), (t1t_ref, k1_ref, True)):
        for dz in range(3):
            for dx in range(3):
                spread = [mm(source[tap(dx, dy, dz, flip)], tile24) for dy in range(3)]
                both = []
                for ch in range(2):
                    value = jnp.zeros((8, 256), F32)
                    for dy in range(3):
                        value = jnp.where(window8 == dy, spread[dy][ch : ch + 1], value)
                    both.append(value)
                target[dz * 16 : dz * 16 + 16, dx * 256 : dx * 256 + 256] = jnp.concatenate(
                    both, 0
                ).astype(BF16)


def join_z(parts, rows, half, at_low, at_high):
    lanes = slice(half * NZ, half * NZ + NZ)
    before = jnp.where(at_low, 0.0, pltpu.roll(parts[0:rows, lanes], 1, 1))
    after = jnp.where(at_high, 0.0, pltpu.roll(parts[2 * rows : 3 * rows, lanes], NZ - 1, 1))
    return parts[rows : 2 * rows, lanes] + (before + after)


def denoise_kernel(
    planes_ref,
    all_ref,
    send_ref,
    mine_ref,
    theirs_ref,
    pair_ref,
    image,
    cots,
    a1,
    s1,
    a2,
    e2,
    e1,
):
    t2_ref, t2t_ref = all_ref.at[0:576, 0:768], all_ref.at[576:1152, 0:768]
    t1_ref, t3t_ref = all_ref.at[0:576, 768:896], all_ref.at[576:1152, 768:896]
    t3_ref, t1t_ref = all_ref.at[1152:1200, 0:768], all_ref.at[1200:1248, 0:768]
    coil, slab = lax.axis_index("coil"), lax.axis_index("slab")
    base, side = 2 * (slab // 2), slab % 2

    def inside(plane):
        return (plane >= 0) & (plane < 16)

    for j in range(10):
        plane = base - 4 + j
        keep = inside(plane)
        source = jnp.clip(plane, 0, 15)
        for ch in range(2):
            image[j, ch, 0:PART_ROWS] = jnp.where(keep, planes_ref[source, ch].astype(F32), 0.0)
            image[j, ch, PART_ROWS:32] = jnp.zeros((8, NZ), F32)
        if 1 <= j < 9:
            for ch in range(4):
                cots[j - 1, ch, 0:PART_ROWS] = jnp.where(
                    keep, planes_ref[source, 2 + ch].astype(F32), 0.0
                )
                cots[j - 1, ch, PART_ROWS:32] = jnp.zeros((8, NZ), F32)

    def at_edges(rows):
        column = lax.broadcasted_iota(jnp.int32, (rows, NZ), 1)
        return column == 0, column == NZ - 1

    for j in range(8):
        a1[j, 576:640] = jnp.zeros((64, NZ), BF16)
        s1[j, 576:640] = jnp.zeros((64, NZ), F32)
    for j in range(6):
        e2[j, 480:640] = jnp.zeros((160, 2 * NZ), BF16)

    def rows_of(table_ref, rows, depth=768):
        if rows == 192:
            return table_ref[:, 0:depth]
        return jnp.concatenate(
            [table_ref[192 * dz : 192 * dz + rows, 0:depth] for dz in range(3)], 0
        )

    def first_step(step, carry):
        pair, block = 2 * (step // 3), step % 3
        at = pl.multiple_of(8 * block, 8)
        to = pl.multiple_of(192 * block, 192)
        pieces = []
        for dx in range(3):
            for ch in range(2):
                pieces.append(
                    jnp.concatenate(
                        [
                            image[pair + dx, ch, pl.ds(at, 16)],
                            image[pair + dx + 1, ch, pl.ds(at, 16)],
                        ],
                        1,
                    ).astype(BF16)
                )
        parts = mm(t1_ref[:, 0:96], jnp.concatenate(pieces, 0))
        low, high = at_edges(192)
        for half in range(2):
            pre = join_z(parts, 192, half, low, high)
            gate = jax.nn.sigmoid(pre)
            a1[pair + half, pl.ds(to, 192)] = (pre * gate).astype(BF16)
            s1[pair + half, pl.ds(to, 192)] = gate * (1.0 + pre * (1.0 - gate))
        return carry

    lax.fori_loop(0, 12, first_step, 0, unroll=6)

    def clear(ref, planes, offset, top, bottom):
        rows, width = ref.shape[1], ref.shape[2]
        for j in range(planes):

            @pl.when(jnp.logical_not(inside(base + offset + j)))
            def _():
                ref[j] = jnp.zeros((rows, width), BF16)

        @pl.when((coil == 0) & (side == 0))
        def _():
            for j in range(planes):
                ref[j, 0:top] = jnp.zeros((top, width), BF16)

        @pl.when((coil == 7) & (side == 1))
        def _():
            for j in range(planes):
                ref[j, bottom:rows] = jnp.zeros((rows - bottom, width), BF16)

    clear(a1, 8, -3, 72, 456)

    def second_block(pair, at, to, rows):
        stacked = jnp.concatenate(
            [
                jnp.concatenate(
                    [a1[pair + dx, pl.ds(to, 256)], a1[pair + dx + 1, pl.ds(to, 256)]], 1
                )
                for dx in range(3)
            ],
            0,
        )
        parts = mm(rows_of(t2_ref, rows), stacked)
        low, high = at_edges(rows)
        for half in range(2):
            pre = join_z(parts, rows, half, low, high)
            gate = jax.nn.sigmoid(pre)
            a2[pair + half, pl.ds(to, rows)] = (pre * gate).astype(BF16)
            slope = gate * (1.0 + pre * (1.0 - gate))
            pieces = []
            for dx in range(3):
                for ch in range(2):
                    pieces.append(
                        jnp.concatenate(
                            [
                                cots[pair + half + dx, ch, pl.ds(at, 16)],
                                cots[pair + half + dx, 2 + ch, pl.ds(at, 16)],
                            ],
                            1,
                        ).astype(BF16)
                    )
            back = mm(rows_of(t3t_ref, rows, 96), jnp.concatenate(pieces, 0))
            for which in range(2):
                grad = join_z(back, rows, which, low, high) * slope
                e2[pair + half, pl.ds(to, rows), which * NZ : which * NZ + NZ] = grad.astype(BF16)

    def second_step(step, carry):
        pair = 2 * step
        second_block(pair, 0, 0, 192)
        second_block(pair, 8, 192, 192)
        second_block(pair, 16, 384, 96)
        return carry

    lax.fori_loop(0, 3, second_step, 0)
    clear(a2, 6, -2, 48, 432)
    clear(e2, 6, -2, 48, 432)

    def third_block(plane, to, rows):
        stacked = jnp.concatenate([e2[plane + dx, pl.ds(to, 256)] for dx in range(3)], 0)
        back = mm(rows_of(t2t_ref, rows), stacked)
        low, high = at_edges(rows)
        slope = s1[plane + 2, pl.ds(to + 48, rows)]
        for which in range(2):
            grad = join_z(back, rows, which, low, high) * slope
            e1[plane, pl.ds(to, rows), which * NZ : which * NZ + NZ] = grad.astype(BF16)

    def third_step(step, carry):
        for plane in (2 * step, 2 * step + 1):
            third_block(plane, 0, 192)
            third_block(plane, 192, 192)
            third_block(plane, 384, 48)
        return carry

    lax.fori_loop(0, 2, third_step, 0)
    for j in range(4):
        e1[j, 432:448] = jnp.zeros((16, 2 * NZ), BF16)
    clear(e1, 4, -1, 24, 408)

    low, high = at_edges(16)
    for block in range(2):
        rows = slice(8 * block, 8 * block + 8)
        window = slice(24 + 192 * block, 280 + 192 * block)
        stacked = jnp.concatenate(
            [jnp.concatenate([a2[1 + dx, window], a2[2 + dx, window]], 1) for dx in range(3)], 0
        )
        parts = mm(t3_ref[...], stacked)
        for p in range(2):
            update = join_z(parts, 16, p, low, high)
            for ch in range(2):
                pair_ref[p, 4 + ch, rows] = update[8 * ch : 8 * ch + 8]

    for p in range(2):
        for block in range(2):
            rows = slice(8 * block, 8 * block + 8)
            shifted = slice(3 + 8 * block, 11 + 8 * block)
            window = slice(192 * block, 192 * block + 256)
            stacked = jnp.concatenate([e1[p + dx, window] for dx in range(3)], 0)
            back = mm(t1t_ref[...], stacked)
            for which in range(2):
                grad = join_z(back, 16, which, low, high)
                for ch in range(2):
                    pair_ref[p, 2 * which + ch, rows] = grad[8 * ch : 8 * ch + 8]
        for ch in range(4):
            pulled = cots[3 + p, ch, 3 : 3 + HALF] + pair_ref[p, ch]
            pulled = pulled.astype(BF16)
            for dest in range(8):
                send_ref[2 * dest + p, ch] = pulled
    mine_ref[...] = pair_ref[side]
    theirs_ref[...] = pair_ref[1 - side]


def normal_kernel(field_ref, maps_ref, weight_ref, tab_ref, out_ref):
    weight = weight_ref[...]
    map_re, map_im = maps_ref[0], maps_ref[1]
    for which in range(2):
        re = field_ref[:, 2 * which].reshape(NY, NZ).astype(F32)
        im = field_ref[:, 2 * which + 1].reshape(NY, NZ).astype(F32)
        f_re, f_im = forward(map_re * re - map_im * im, map_re * im + map_im * re, tab_ref)
        b_re, b_im = inverse(weight * f_re, weight * f_im, tab_ref)
        out_re = (map_re * b_re + map_im * b_im).astype(BF16)
        out_im = (map_re * b_im - map_im * b_re).astype(BF16)
        for dest in range(8):
            rows = slice(NYL * dest, NYL * dest + NYL)
            out_ref[dest, 2 * which] = out_re[rows]
            out_ref[dest, 2 * which + 1] = out_im[rows]


def final_kernel(
    got_ref, mine_ref, theirs_ref, relaxed_ref, own_ref, loss_ref, new_ref, probe_ref, next_ref
):
    side = lax.axis_index("slab") % 2
    sums = []
    for ch in range(4):
        total = got_ref[0, ch].astype(F32)
        for source in range(1, 8):
            total = total + got_ref[source, ch].astype(F32)
        sums.append(STEP * total)

    def put(first, part_ref):
        rows = slice(first, first + HALF)
        for ch in range(2):
            new_ref[ch, rows] = relaxed_ref[ch, rows] + part_ref[4 + ch]
            probe_ref[ch, rows] = own_ref[2 + ch, rows] + part_ref[ch] - sums[ch][rows]
            pulled = own_ref[4 + ch, rows] + part_ref[2 + ch]
            next_ref[ch, rows] = loss_ref[ch, rows] + (pulled - sums[2 + ch][rows])

    @pl.when(side == 0)
    def _():
        put(0, mine_ref)
        put(HALF, theirs_ref)

    @pl.when(side == 1)
    def _():
        put(0, theirs_ref)
        put(HALF, mine_ref)


def on_device(
    coil_maps,
    kspace,
    sample_mask,
    iterate,
    probe_bits,
    loss_gradient,
    adjoint,
    kernel_first,
    kernel_second,
    kernel_last,
):
    maps = coil_maps[0, :, 0]
    data = kspace[0, :, 0]
    iterate, bits, loss, adj = (a[:, 0] for a in (iterate, probe_bits, loss_gradient, adjoint))
    slabs = lax.axis_size("slab")
    coils = lax.axis_size("coil")
    families = [
        [c * slabs + 2 * j + h for c in range(coils) for h in range(2)] for j in range(slabs // 2)
    ]

    k1 = jnp.transpose(kernel_first, (2, 3, 4, 1, 0)).reshape(27, 2, 24)
    k2 = jnp.transpose(kernel_second, (2, 3, 4, 0, 1)).reshape(27, 24, 24)
    k3 = jnp.transpose(kernel_last, (2, 3, 4, 0, 1)).reshape(27, 2, 24)
    staged = pl.pallas_call(
        stage_kernel,
        compiler_params=GRANT,
        out_shape=[
            jax.ShapeDtypeStruct((2, NY, NZ), F32),
            jax.ShapeDtypeStruct((2, NY, NZ), F32),
            jax.ShapeDtypeStruct((NY, NZ), F32),
            jax.ShapeDtypeStruct((6, NYL, NZ), F32),
            jax.ShapeDtypeStruct((48, NZ), BF16),
            jax.ShapeDtypeStruct((1536, 256), BF16),
            jax.ShapeDtypeStruct((8, 2, NYL, NZ), BF16),
            jax.ShapeDtypeStruct((1248, 896), BF16),
        ],
        in_specs=[pl.BlockSpec(memory_space=pltpu.HBM)] * 10,
        out_specs=whole(8),
        scratch_shapes=[
            pltpu.VMEM((NY, NZ), jnp.int32),
            pltpu.VMEM((2, NYL, NZ), jnp.int32),
            pltpu.VMEM((27, 2, 24), BF16),
            pltpu.VMEM((27, 24, 24), BF16),
            pltpu.VMEM((27, 2, 24), BF16),
            pltpu.SemaphoreType.DMA((10,)),
        ],
    )(
        *(
            pltpu.with_memory_space_constraint(x, pltpu.HBM)
            for x in (
                maps, data, sample_mask, iterate, bits, adj, fourier_constants(), k1, k2, k3
            )
        )
    )
    maps, masked, weight, own, edges, fourier, first, toeplitz = staged
    field = lax.all_to_all(first, "coil", 0, 0)
    partial_sums = pl.pallas_call(
        gradient_kernel,
        compiler_params=GRANT,
        out_shape=jax.ShapeDtypeStruct((8, 128, NZ), BF16),
        in_specs=whole(6),
        out_specs=whole(1)[0],
        scratch_shapes=[pltpu.VMEM((2, NY + 8, NZ), F32)],
    )(field, maps, masked, weight, edges, fourier)
    got = lax.all_to_all(partial_sums, "coil", 0, 0)
    payload, relaxed = pl.pallas_call(
        relax_kernel,
        compiler_params=GRANT,
        out_shape=[
            jax.ShapeDtypeStruct((16, 6, PART_ROWS, NZ), BF16),
            jax.ShapeDtypeStruct((2, NYL, NZ), F32),
        ],
        in_specs=whole(3),
        out_specs=whole(2),
        scratch_shapes=[
            pltpu.VMEM((2, HALO_ROWS, NZ), F32),
            pltpu.VMEM((4, HALO_ROWS, NZ), F32),
        ],
    )(got, field, own)
    planes = lax.all_to_all(payload, "slab", 0, 0)
    send, mine, theirs = pl.pallas_call(
        denoise_kernel,
        compiler_params=GRANT,
        out_shape=[
            jax.ShapeDtypeStruct((16, 4, HALF, NZ), BF16),
            jax.ShapeDtypeStruct((6, HALF, NZ), F32),
            jax.ShapeDtypeStruct((6, HALF, NZ), F32),
        ],
        in_specs=whole(2),
        out_specs=whole(3),
        scratch_shapes=[
            pltpu.VMEM((2, 6, HALF, NZ), F32),
            pltpu.VMEM((10, 2, 32, NZ), F32),
            pltpu.VMEM((8, 4, 32, NZ), F32),
            pltpu.VMEM((8, 640, NZ), BF16),
            pltpu.VMEM((8, 640, NZ), F32),
            pltpu.VMEM((6, 480, NZ), BF16),
            pltpu.VMEM((6, 640, 2 * NZ), BF16),
            pltpu.VMEM((4, 448, 2 * NZ), BF16),
        ],
    )(planes, toeplitz)
    spread = lax.all_to_all(send, ("coil", "slab"), 0, 0, axis_index_groups=families)
    theirs = lax.ppermute(theirs, "slab", [(i, i + 1 - 2 * (i % 2)) for i in range(slabs)])
    back = pl.pallas_call(
        normal_kernel,
        compiler_params=GRANT,
        out_shape=jax.ShapeDtypeStruct((8, 4, NYL, NZ), BF16),
        in_specs=whole(4),
        out_specs=whole(1)[0],
    )(spread, maps, weight, fourier)
    back = lax.all_to_all(back, "coil", 0, 0)
    new_iterate, probe, following = pl.pallas_call(
        final_kernel,
        compiler_params=GRANT,
        out_shape=[jax.ShapeDtypeStruct((2, NYL, NZ), F32)] * 3,
        in_specs=whole(6),
        out_specs=whole(3),
    )(back, mine, theirs, relaxed, own, loss)
    return new_iterate[:, None], probe[:, None], following[:, None]


def solution(mesh):
    image = P(None, "slab", "coil", None)
    coils = P("coil", None, "slab", None, None)
    return jax.shard_map(
        on_device,
        mesh=mesh,
        in_specs=(coils, coils, P(), image, image, image, image, P(), P(), P()),
        out_specs=(image, image, image),
        check_vma=False,
    )
```

```python
import math

import jax
import jax.numpy as jnp
import numpy as np
from jax import lax
from jax.experimental import pallas as pl
from jax.experimental.pallas import tpu as pltpu
from jax.sharding import PartitionSpec as P

STEP = 0.8
F32 = jnp.float32
BF16 = jnp.bfloat16
NZ = 128
NY = 256
NYL = 32
HALO_ROWS = 40
HALF = 16
PART_ROWS = 24
GRANT = pltpu.CompilerParams(vmem_limit_bytes=24 << 20)


def whole(count):
    return [pl.BlockSpec(memory_space=pltpu.VMEM)] * count


def split_host(table):
    high = table.astype(np.float32).astype(jnp.bfloat16)
    low = (table - high.astype(np.float64)).astype(jnp.bfloat16)
    return high, low


def fourier_constants():
    def cos_sin(length):
        index = np.arange(length)
        angles = (index[:, None] * index[None, :] % length) * (2.0 * math.pi / length)
        return np.cos(angles) / math.sqrt(length), np.sin(angles) / math.sqrt(length)

    cos_y, sin_y = cos_sin(NY)
    cos_z, sin_z = cos_sin(NZ)
    along_y = np.concatenate([cos_y, sin_y], axis=0)
    along_z = np.block([[cos_z, -sin_z], [sin_z, cos_z]])
    return jnp.asarray(np.concatenate(split_host(along_y) + split_host(along_z), axis=0))


def split(values):
    high = values.astype(BF16)
    return high, (values - high.astype(F32)).astype(BF16)


def mm(left, right):
    return jnp.dot(left, right, preferred_element_type=F32)


def along_z(joined, tab_ref):
    high, low = split(joined)
    z_high, z_low = tab_ref[1024:1280], tab_ref[1280:1536]
    return mm(high, z_high) + (mm(high, z_low) + mm(low, z_high))


def along_y(joined, tab_ref):
    high, low = split(joined)
    y_high, y_low = tab_ref[0:512], tab_ref[512:1024]
    return mm(y_high, high) + (mm(y_low, high) + mm(y_high, low))


def forward(real, imag, tab_ref):
    turned = along_y(along_z(jnp.concatenate([real, imag], 1), tab_ref), tab_ref)
    cos_part, sin_part = turned[:NY], turned[NY:]
    return cos_part[:, :NZ] + sin_part[:, NZ:], cos_part[:, NZ:] - sin_part[:, :NZ]


def inverse(real, imag, tab_ref):
    turned = along_y(jnp.concatenate([real, imag], 1), tab_ref)
    cos_part, sin_part = turned[:NY], turned[NY:]
    back = cos_part[:, :NZ] - sin_part[:, NZ:], -(cos_part[:, NZ:] + sin_part[:, :NZ])
    turned = along_z(jnp.concatenate(back, 1), tab_ref)
    return turned[:, :NZ], -turned[:, NZ:]


def stage_kernel(
    maps_in,
    kspace_in,
    mask_in,
    iterate_in,
    bits_in,
    adj_in,
    tab_in,
    k1_in,
    k2_in,
    k3_in,
    maps_ref,
    masked_ref,
    weight_ref,
    own_ref,
    edges_ref,
    tab_ref,
    first_ref,
    all_ref,
    mask_ref,
    bits_ref,
    k1_ref,
    k2_ref,
    k3_ref,
    sems,
):
    moves = (
        (k1_in, k1_ref),
        (k2_in, k2_ref),
        (k3_in, k3_ref),
        (iterate_in, own_ref.at[0:2]),
        (bits_in, bits_ref),
        (adj_in, own_ref.at[4:6]),
        (mask_in, mask_ref),
        (kspace_in, masked_ref),
        (maps_in, maps_ref),
        (tab_in, tab_ref),
    )
    copies = [pltpu.make_async_copy(s, d, sems.at[i]) for i, (s, d) in enumerate(moves)]
    for copy in copies:
        copy.start()
    for copy in copies[0:3]:
        copy.wait()
    build_tables(k1_ref, k2_ref, k3_ref, all_ref)
    for copy in copies[3:]:
        copy.wait()
    for ch in range(2):
        rows = own_ref[ch].astype(BF16)
        for dest in range(8):
            first_ref[dest, ch] = rows
    weight = mask_ref[...].astype(F32)
    weight_ref[...] = weight
    for ch in range(2):
        masked_ref[ch] = weight * masked_ref[ch]
        own_ref[2 + ch] = (2 * bits_ref[ch] - 1).astype(F32)
    edges = []
    for ch in (2, 3, 4, 5, 0, 1):
        rows = own_ref[ch]
        if ch < 2:
            rows = split(rows)[1].astype(F32)
        edges += [rows[0:4], rows[NYL - 4 : NYL]]
    edges_ref[...] = jnp.concatenate(edges, 0).astype(BF16)


def gradient_kernel(
    field_ref, maps_ref, masked_ref, weight_ref, edges_ref, tab_ref, out_ref, pad
):
    weight = weight_ref[...]
    map_re, map_im = maps_ref[0], maps_ref[1]
    re = field_ref[:, 0].astype(F32).reshape(NY, NZ)
    im = field_ref[:, 1].astype(F32).reshape(NY, NZ)
    f_re, f_im = forward(map_re * re - map_im * im, map_re * im + map_im * re, tab_ref)
    f_re = weight * f_re - masked_ref[0]
    f_im = weight * f_im - masked_ref[1]
    b_re, b_im = inverse(f_re, f_im, tab_ref)
    zero = jnp.zeros((4, NZ), F32)
    for ch in range(2):
        pad[ch, 0:4] = zero
        pad[ch, NY + 4 : NY + 8] = zero
    pad[0, 4 : NY + 4] = map_re * b_re + map_im * b_im
    pad[1, 4 : NY + 4] = map_re * b_im - map_im * b_re
    edges = edges_ref[...]
    for dest in range(8):
        for ch in range(2):
            out_ref[dest, HALO_ROWS * ch : HALO_ROWS * ch + HALO_ROWS] = pad[
                ch, NYL * dest : NYL * dest + HALO_ROWS
            ].astype(BF16)
        out_ref[dest, 80:128] = edges


def relax_kernel(got_ref, field_ref, own_ref, out_ref, relaxed_ref, pad, qpad):
    coil = lax.axis_index("coil")
    lower, upper = jnp.maximum(coil - 1, 0), jnp.minimum(coil + 1, 7)
    below = jnp.where(coil > 0, got_ref[lower, 80:128].astype(F32), 0.0)
    above = jnp.where(coil < 7, got_ref[upper, 80:128].astype(F32), 0.0)
    for ch in range(2):
        under = jnp.where(coil > 0, field_ref[lower, ch].astype(F32), 0.0)
        over = jnp.where(coil < 7, field_ref[upper, ch].astype(F32), 0.0)
        at = 32 + 8 * ch
        pad[ch, 0:4] = under[NYL - 4 : NYL] + below[at + 4 : at + 8]
        pad[ch, 4 : 4 + NYL] = own_ref[ch]
        pad[ch, 4 + NYL : HALO_ROWS] = over[0:4] + above[at : at + 4]
        rows = slice(HALO_ROWS * ch, HALO_ROWS * ch + HALO_ROWS)
        total = got_ref[0, rows].astype(F32)
        for source in range(1, 8):
            total = total + got_ref[source, rows].astype(F32)
        relaxed = pad[ch] - STEP * total
        relaxed_ref[ch] = relaxed[4 : 4 + NYL]
        rows = relaxed.astype(BF16)
        for dest in range(16):
            first = HALF * (dest % 2)
            out_ref[dest, ch] = rows[first : first + PART_ROWS]
    for ch in range(4):
        qpad[ch, 0:3] = below[ch * 8 + 5 : ch * 8 + 8]
        qpad[ch, 3 : 3 + NYL] = own_ref[2 + ch]
        qpad[ch, 3 + NYL : 7 + NYL] = above[ch * 8 : ch * 8 + 4]
        qpad[ch, 7 + NYL : HALO_ROWS] = jnp.zeros((1, NZ), F32)
        rows = qpad[ch].astype(BF16)
        for dest in range(16):
            first = HALF * (dest % 2)
            out_ref[dest, 2 + ch] = rows[first : first + PART_ROWS]


def dot_first(left, right):
    return lax.dot_general(left, right, (((0,), (0,)), ((), ())), preferred_element_type=F32)


def build_tables(k1_ref, k2_ref, k3_ref, all_ref):
    t2_ref, t2t_ref = all_ref.at[0:576, 0:768], all_ref.at[576:1152, 0:768]
    t1_ref, t3t_ref = all_ref.at[0:192, 768:1152], all_ref.at[192:384, 768:1152]
    t3_ref, t1t_ref = all_ref.at[1152:1200, 0:768], all_ref.at[1200:1248, 0:768]
    lane = lax.broadcasted_iota(jnp.int32, (24, 256), 1)
    row = lax.broadcasted_iota(jnp.int32, (24, 256), 0)
    tile24 = ((lane % 24 == row) & (lane < 240)).astype(BF16)
    window = jnp.where(lane < 240, lane // 24, 99)

    def tap(dx, dy, dz, flip):
        if flip:
            dx, dy, dz = 2 - dx, 2 - dy, 2 - dz
        return dx * 9 + dy * 3 + dz

    for target, flip in ((t2_ref, False), (t2t_ref, True)):
        for dz in range(3):
            for dx in range(3):
                spread = []
                for dy in range(3):
                    block = k2_ref[tap(dx, dy, dz, flip)]
                    spread.append(dot_first(block, tile24) if flip else mm(block, tile24))
                for yo in range(8):
                    value = jnp.zeros((24, 256), F32)
                    for dy in range(3):
                        value = jnp.where(window == yo + dy, spread[dy], value)
                    at = dz * 192 + yo * 24
                    target[at : at + 24, dx * 256 : dx * 256 + 256] = value.astype(BF16)

    lane = lax.broadcasted_iota(jnp.int32, (24, 384), 1)
    lane2 = lax.broadcasted_iota(jnp.int32, (2, 384), 1)
    row2 = lax.broadcasted_iota(jnp.int32, (2, 384), 0)
    tile2 = ((lane2 // 16) % 2 == row2).astype(BF16)
    group, offset = lane // 32, lane % 16
    for target, source, flip in ((t1_ref, k1_ref, False), (t3t_ref, k3_ref, True)):
        spread = []
        for dy in range(3):
            value = jnp.zeros((24, 384), F32)
            for dx in range(3):
                for dz in range(3):
                    block = dot_first(source[tap(dx, dy, dz, flip)], tile2)
                    value = jnp.where(group == dx * 3 + dz, block, value)
            spread.append(value)
        for yo in range(8):
            value = jnp.zeros((24, 384), F32)
            for dy in range(3):
                value = jnp.where(offset == yo + dy, spread[dy], value)
            target[yo * 24 : yo * 24 + 24, :] = value.astype(BF16)

    window8 = window[0:8] - lax.broadcasted_iota(jnp.int32, (8, 256), 0)
    for target, source, flip in ((t3_ref, k3_ref, False), (t1t_ref, k1_ref, True)):
        for dz in range(3):
            for dx in range(3):
                spread = [mm(source[tap(dx, dy, dz, flip)], tile24) for dy in range(3)]
                both = []
                for ch in range(2):
                    value = jnp.zeros((8, 256), F32)
                    for dy in range(3):
                        value = jnp.where(window8 == dy, spread[dy][ch : ch + 1], value)
                    both.append(value)
                target[dz * 16 : dz * 16 + 16, dx * 256 : dx * 256 + 256] = jnp.concatenate(
                    both, 0
                ).astype(BF16)


def join_z(parts, rows, half, at_low, at_high):
    lanes = slice(half * NZ, half * NZ + NZ)
    before = jnp.where(at_low, 0.0, pltpu.roll(parts[0:rows, lanes], 1, 1))
    after = jnp.where(at_high, 0.0, pltpu.roll(parts[2 * rows : 3 * rows, lanes], NZ - 1, 1))
    return parts[rows : 2 * rows, lanes] + (before + after)


def denoise_kernel(
    planes_ref,
    all_ref,
    send_ref,
    mine_ref,
    theirs_ref,
    pair_ref,
    image,
    cots,
    a1,
    s1,
    a2,
    e2,
    e1,
):
    t2_ref, t2t_ref = all_ref.at[0:576, 0:768], all_ref.at[576:1152, 0:768]
    t1_ref, t3t_ref = all_ref.at[0:192, 768:1152], all_ref.at[192:384, 768:1152]
    t3_ref, t1t_ref = all_ref.at[1152:1200, 0:768], all_ref.at[1200:1248, 0:768]
    coil, slab = lax.axis_index("coil"), lax.axis_index("slab")
    base, side = 2 * (slab // 2), slab % 2

    def inside(plane):
        return (plane >= 0) & (plane < 16)

    def at_edges(rows):
        column = lax.broadcasted_iota(jnp.int32, (rows, NZ), 1)
        return column == 0, column == NZ - 1

    low, high = at_edges(PART_ROWS)

    def stage(ref, j, ch, rows):
        ref[0, j, ch, 0:PART_ROWS] = jnp.where(low, 0.0, pltpu.roll(rows, 1, 1))
        ref[1, j, ch, 0:PART_ROWS] = rows
        ref[2, j, ch, 0:PART_ROWS] = jnp.where(high, 0.0, pltpu.roll(rows, NZ - 1, 1))
        for dz in range(3):
            ref[dz, j, ch, PART_ROWS:32] = jnp.zeros((8, NZ), F32)

    for j in range(10):
        plane = base - 4 + j
        keep = inside(plane)
        source = jnp.clip(plane, 0, 15)
        for ch in range(2):
            stage(image, j, ch, jnp.where(keep, planes_ref[source, ch].astype(F32), 0.0))
        if 1 <= j < 9:
            for ch in range(4):
                rows = jnp.where(keep, planes_ref[source, 2 + ch].astype(F32), 0.0)
                stage(cots, j - 1, ch, rows)

    def usable(plane):
        return jnp.where(inside(plane), 1.0, 0.0)

    for j in range(8):
        a1[j, 576:640] = jnp.zeros((64, NZ), BF16)
        s1[j, 576:640] = jnp.zeros((64, NZ), F32)
    for j in range(6):
        e2[j, 480:640] = jnp.zeros((160, 2 * NZ), BF16)

    def rows_of(table_ref, rows):
        if rows == 192:
            return table_ref[...]
        return jnp.concatenate([table_ref[192 * dz : 192 * dz + rows] for dz in range(3)], 0)

    def first_step(step, carry):
        pair, block = 2 * (step // 3), step % 3
        at = pl.multiple_of(8 * block, 8)
        to = pl.multiple_of(192 * block, 192)
        pieces = []
        for dx in range(3):
            for dz in range(3):
                for ch in range(2):
                    pieces.append(
                        jnp.concatenate(
                            [
                                image[dz, pair + dx, ch, pl.ds(at, 16)],
                                image[dz, pair + dx + 1, ch, pl.ds(at, 16)],
                            ],
                            1,
                        ).astype(BF16)
                    )
        both = mm(t1_ref[:, 0:288], jnp.concatenate(pieces, 0))
        for half in range(2):
            pre = both[:, half * NZ : half * NZ + NZ]
            gate = jax.nn.sigmoid(pre)
            keep = usable(base - 3 + pair + half)
            a1[pair + half, pl.ds(to, 192)] = (pre * gate * keep).astype(BF16)
            s1[pair + half, pl.ds(to, 192)] = gate * (1.0 + pre * (1.0 - gate)) * keep
        return carry

    lax.fori_loop(0, 12, first_step, 0, unroll=12)

    def clear(ref, planes, top, bottom):
        rows = ref.shape[1]
        first, last = (coil == 0) & (side == 0), (coil == 7) & (side == 1)
        for j in range(planes):
            value = ref[j, 0:top]
            ref[j, 0:top] = jnp.where(first, jnp.zeros_like(value), value)
            value = ref[j, bottom:rows]
            ref[j, bottom:rows] = jnp.where(last, jnp.zeros_like(value), value)

    clear(a1, 8, 72, 456)

    def second_block(pair, at, to, rows):
        stacked = jnp.concatenate(
            [
                jnp.concatenate(
                    [a1[pair + dx, pl.ds(to, 256)], a1[pair + dx + 1, pl.ds(to, 256)]], 1
                )
                for dx in range(3)
            ],
            0,
        )
        parts = mm(rows_of(t2_ref, rows), stacked)
        low, high = at_edges(rows)
        for half in range(2):
            pre = join_z(parts, rows, half, low, high)
            gate = jax.nn.sigmoid(pre)
            keep = usable(base - 2 + pair + half)
            a2[pair + half, pl.ds(to, rows)] = (pre * gate * keep).astype(BF16)
            slope = gate * (1.0 + pre * (1.0 - gate)) * keep
            pieces = []
            for dx in range(3):
                for dz in range(3):
                    for ch in range(2):
                        pieces.append(
                            jnp.concatenate(
                                [
                                    cots[dz, pair + half + dx, ch, pl.ds(at, 16)],
                                    cots[dz, pair + half + dx, 2 + ch, pl.ds(at, 16)],
                                ],
                                1,
                            ).astype(BF16)
                        )
            back = mm(t3t_ref[0:rows, 0:288], jnp.concatenate(pieces, 0))
            for which in range(2):
                lanes = slice(which * NZ, which * NZ + NZ)
                e2[pair + half, pl.ds(to, rows), lanes] = (back[:, lanes] * slope).astype(BF16)

    def second_step(step, carry):
        pair = 2 * step
        second_block(pair, 0, 0, 192)
        second_block(pair, 8, 192, 192)
        second_block(pair, 16, 384, 96)
        return carry

    lax.fori_loop(0, 3, second_step, 0, unroll=3)
    clear(a2, 6, 48, 432)
    clear(e2, 6, 48, 432)

    def third_block(plane, to, rows):
        stacked = jnp.concatenate([e2[plane + dx, pl.ds(to, 256)] for dx in range(3)], 0)
        back = mm(rows_of(t2t_ref, rows), stacked)
        low, high = at_edges(rows)
        slope = s1[plane + 2, pl.ds(to + 48, rows)]
        for which in range(2):
            grad = join_z(back, rows, which, low, high) * slope
            e1[plane, pl.ds(to, rows), which * NZ : which * NZ + NZ] = grad.astype(BF16)

    def third_step(step, carry):
        for plane in (2 * step, 2 * step + 1):
            third_block(plane, 0, 192)
            third_block(plane, 192, 192)
            third_block(plane, 384, 48)
        return carry

    lax.fori_loop(0, 2, third_step, 0, unroll=2)
    for j in range(4):
        e1[j, 432:448] = jnp.zeros((16, 2 * NZ), BF16)
    clear(e1, 4, 24, 408)

    low, high = at_edges(16)
    for block in range(2):
        rows = slice(8 * block, 8 * block + 8)
        window = slice(24 + 192 * block, 280 + 192 * block)
        stacked = jnp.concatenate(
            [jnp.concatenate([a2[1 + dx, window], a2[2 + dx, window]], 1) for dx in range(3)], 0
        )
        parts = mm(t3_ref[...], stacked)
        for p in range(2):
            update = join_z(parts, 16, p, low, high)
            for ch in range(2):
                pair_ref[p, 4 + ch, rows] = update[8 * ch : 8 * ch + 8]

    for p in range(2):
        for block in range(2):
            rows = slice(8 * block, 8 * block + 8)
            shifted = slice(3 + 8 * block, 11 + 8 * block)
            window = slice(192 * block, 192 * block + 256)
            stacked = jnp.concatenate([e1[p + dx, window] for dx in range(3)], 0)
            back = mm(t1t_ref[...], stacked)
            for which in range(2):
                grad = join_z(back, 16, which, low, high)
                for ch in range(2):
                    pair_ref[p, 2 * which + ch, rows] = grad[8 * ch : 8 * ch + 8]
        for ch in range(4):
            pulled = cots[1, 3 + p, ch, 3 : 3 + HALF] + pair_ref[p, ch]
            pulled = pulled.astype(BF16)
            for dest in range(8):
                send_ref[2 * dest + p, ch] = pulled
    mine_ref[...] = pair_ref[side]
    theirs_ref[...] = pair_ref[1 - side]


def normal_kernel(field_ref, maps_ref, weight_ref, tab_ref, out_ref):
    weight = weight_ref[...]
    map_re, map_im = maps_ref[0], maps_ref[1]
    for which in range(2):
        re = field_ref[:, 2 * which].reshape(NY, NZ).astype(F32)
        im = field_ref[:, 2 * which + 1].reshape(NY, NZ).astype(F32)
        f_re, f_im = forward(map_re * re - map_im * im, map_re * im + map_im * re, tab_ref)
        b_re, b_im = inverse(weight * f_re, weight * f_im, tab_ref)
        out_re = (map_re * b_re + map_im * b_im).astype(BF16)
        out_im = (map_re * b_im - map_im * b_re).astype(BF16)
        for dest in range(8):
            rows = slice(NYL * dest, NYL * dest + NYL)
            out_ref[dest, 2 * which] = out_re[rows]
            out_ref[dest, 2 * which + 1] = out_im[rows]


def final_kernel(
    got_ref, mine_ref, theirs_ref, relaxed_ref, own_ref, loss_ref, new_ref, probe_ref, next_ref
):
    side = lax.axis_index("slab") % 2
    sums = []
    for ch in range(4):
        total = got_ref[0, ch].astype(F32)
        for source in range(1, 8):
            total = total + got_ref[source, ch].astype(F32)
        sums.append(STEP * total)

    def put(first, part_ref):
        rows = slice(first, first + HALF)
        for ch in range(2):
            new_ref[ch, rows] = relaxed_ref[ch, rows] + part_ref[4 + ch]
            probe_ref[ch, rows] = own_ref[2 + ch, rows] + part_ref[ch] - sums[ch][rows]
            pulled = own_ref[4 + ch, rows] + part_ref[2 + ch]
            next_ref[ch, rows] = loss_ref[ch, rows] + (pulled - sums[2 + ch][rows])

    @pl.when(side == 0)
    def _():
        put(0, mine_ref)
        put(HALF, theirs_ref)

    @pl.when(side == 1)
    def _():
        put(0, theirs_ref)
        put(HALF, mine_ref)


def on_device(
    coil_maps,
    kspace,
    sample_mask,
    iterate,
    probe_bits,
    loss_gradient,
    adjoint,
    kernel_first,
    kernel_second,
    kernel_last,
):
    maps = coil_maps[0, :, 0]
    data = kspace[0, :, 0]
    iterate, bits, loss, adj = (a[:, 0] for a in (iterate, probe_bits, loss_gradient, adjoint))
    slabs = lax.axis_size("slab")
    coils = lax.axis_size("coil")
    families = [
        [c * slabs + 2 * j + h for c in range(coils) for h in range(2)] for j in range(slabs // 2)
    ]

    k1 = jnp.transpose(kernel_first, (2, 3, 4, 1, 0)).reshape(27, 2, 24)
    k2 = jnp.transpose(kernel_second, (2, 3, 4, 0, 1)).reshape(27, 24, 24)
    k3 = jnp.transpose(kernel_last, (2, 3, 4, 0, 1)).reshape(27, 2, 24)
    staged = pl.pallas_call(
        stage_kernel,
        compiler_params=GRANT,
        out_shape=[
            jax.ShapeDtypeStruct((2, NY, NZ), F32),
            jax.ShapeDtypeStruct((2, NY, NZ), F32),
            jax.ShapeDtypeStruct((NY, NZ), F32),
            jax.ShapeDtypeStruct((6, NYL, NZ), F32),
            jax.ShapeDtypeStruct((48, NZ), BF16),
            jax.ShapeDtypeStruct((1536, 256), BF16),
            jax.ShapeDtypeStruct((8, 2, NYL, NZ), BF16),
            jax.ShapeDtypeStruct((1248, 1152), BF16),
        ],
        in_specs=[pl.BlockSpec(memory_space=pltpu.HBM)] * 10,
        out_specs=whole(8),
        scratch_shapes=[
            pltpu.VMEM((NY, NZ), jnp.int32),
            pltpu.VMEM((2, NYL, NZ), jnp.int32),
            pltpu.VMEM((27, 2, 24), BF16),
            pltpu.VMEM((27, 24, 24), BF16),
            pltpu.VMEM((27, 2, 24), BF16),
            pltpu.SemaphoreType.DMA((10,)),
        ],
    )(
        *(
            pltpu.with_memory_space_constraint(x, pltpu.HBM)
            for x in (
                maps, data, sample_mask, iterate, bits, adj, fourier_constants(), k1, k2, k3
            )
        )
    )
    maps, masked, weight, own, edges, fourier, first, toeplitz = staged
    field = lax.all_to_all(first, "coil", 0, 0)
    partial_sums = pl.pallas_call(
        gradient_kernel,
        compiler_params=GRANT,
        out_shape=jax.ShapeDtypeStruct((8, 128, NZ), BF16),
        in_specs=whole(6),
        out_specs=whole(1)[0],
        scratch_shapes=[pltpu.VMEM((2, NY + 8, NZ), F32)],
    )(field, maps, masked, weight, edges, fourier)
    got = lax.all_to_all(partial_sums, "coil", 0, 0)
    payload, relaxed = pl.pallas_call(
        relax_kernel,
        compiler_params=GRANT,
        out_shape=[
            jax.ShapeDtypeStruct((16, 6, PART_ROWS, NZ), BF16),
            jax.ShapeDtypeStruct((2, NYL, NZ), F32),
        ],
        in_specs=whole(3),
        out_specs=whole(2),
        scratch_shapes=[
            pltpu.VMEM((2, HALO_ROWS, NZ), F32),
            pltpu.VMEM((4, HALO_ROWS, NZ), F32),
        ],
    )(got, field, own)
    planes = lax.all_to_all(payload, "slab", 0, 0)
    send, mine, theirs = pl.pallas_call(
        denoise_kernel,
        compiler_params=GRANT,
        out_shape=[
            jax.ShapeDtypeStruct((16, 4, HALF, NZ), BF16),
            jax.ShapeDtypeStruct((6, HALF, NZ), F32),
            jax.ShapeDtypeStruct((6, HALF, NZ), F32),
        ],
        in_specs=whole(2),
        out_specs=whole(3),
        scratch_shapes=[
            pltpu.VMEM((2, 6, HALF, NZ), F32),
            pltpu.VMEM((3, 10, 2, 32, NZ), F32),
            pltpu.VMEM((3, 8, 4, 32, NZ), F32),
            pltpu.VMEM((8, 640, NZ), BF16),
            pltpu.VMEM((8, 640, NZ), F32),
            pltpu.VMEM((6, 480, NZ), BF16),
            pltpu.VMEM((6, 640, 2 * NZ), BF16),
            pltpu.VMEM((4, 448, 2 * NZ), BF16),
        ],
    )(planes, toeplitz)
    spread = lax.all_to_all(send, ("coil", "slab"), 0, 0, axis_index_groups=families)
    theirs = lax.ppermute(theirs, "slab", [(i, i + 1 - 2 * (i % 2)) for i in range(slabs)])
    back = pl.pallas_call(
        normal_kernel,
        compiler_params=GRANT,
        out_shape=jax.ShapeDtypeStruct((8, 4, NYL, NZ), BF16),
        in_specs=whole(4),
        out_specs=whole(1)[0],
    )(spread, maps, weight, fourier)
    back = lax.all_to_all(back, "coil", 0, 0)
    new_iterate, probe, following = pl.pallas_call(
        final_kernel,
        compiler_params=GRANT,
        out_shape=[jax.ShapeDtypeStruct((2, NYL, NZ), F32)] * 3,
        in_specs=whole(6),
        out_specs=whole(3),
    )(back, mine, theirs, relaxed, own, loss)
    return new_iterate[:, None], probe[:, None], following[:, None]


def solution(mesh):
    image = P(None, "slab", "coil", None)
    coils = P("coil", None, "slab", None, None)
    return jax.shard_map(
        on_device,
        mesh=mesh,
        in_specs=(coils, coils, P(), image, image, image, image, P(), P(), P()),
        out_specs=(image, image, image),
        check_vma=False,
    )
```

```python
import math

import jax
import jax.numpy as jnp
import numpy as np
from jax import lax
from jax.experimental import pallas as pl
from jax.experimental.pallas import tpu as pltpu
from jax.sharding import PartitionSpec as P

STEP = 0.8
F32 = jnp.float32
BF16 = jnp.bfloat16
NZ = 128
NY = 256
NYL = 32
HALO_ROWS = 40
HALF = 16
PART_ROWS = 24
MESSAGE = 136
GRANT = pltpu.CompilerParams(vmem_limit_bytes=24 << 20)


def whole(count):
    return [pl.BlockSpec(memory_space=pltpu.VMEM)] * count


def split_host(table):
    high = table.astype(np.float32).astype(jnp.bfloat16)
    low = (table - high.astype(np.float64)).astype(jnp.bfloat16)
    return high, low


def fourier_constants():
    def cos_sin(length):
        index = np.arange(length)
        angles = (index[:, None] * index[None, :] % length) * (2.0 * math.pi / length)
        return np.cos(angles) / math.sqrt(length), np.sin(angles) / math.sqrt(length)

    cos_y, sin_y = cos_sin(NY)
    cos_z, sin_z = cos_sin(NZ)
    along_y = np.concatenate([cos_y, sin_y], axis=0)
    along_z = np.block([[cos_z, -sin_z], [sin_z, cos_z]])
    return jnp.asarray(np.concatenate(split_host(along_y) + split_host(along_z), axis=0))


def split(values):
    high = values.astype(BF16)
    return high, (values - high.astype(F32)).astype(BF16)


def mm(left, right):
    return jnp.dot(left, right, preferred_element_type=F32)


def along_z(joined, tab_ref):
    high, low = split(joined)
    z_high, z_low = tab_ref[1024:1280], tab_ref[1280:1536]
    return mm(high, z_high) + (mm(high, z_low) + mm(low, z_high))


def along_y(joined, tab_ref):
    high, low = split(joined)
    y_high, y_low = tab_ref[0:512], tab_ref[512:1024]
    return mm(y_high, high) + (mm(y_low, high) + mm(y_high, low))


def forward(real, imag, tab_ref):
    turned = along_y(along_z(jnp.concatenate([real, imag], 1), tab_ref), tab_ref)
    cos_part, sin_part = turned[:NY], turned[NY:]
    return cos_part[:, :NZ] + sin_part[:, NZ:], cos_part[:, NZ:] - sin_part[:, :NZ]


def inverse(real, imag, tab_ref):
    turned = along_y(jnp.concatenate([real, imag], 1), tab_ref)
    cos_part, sin_part = turned[:NY], turned[NY:]
    back = cos_part[:, :NZ] - sin_part[:, NZ:], -(cos_part[:, NZ:] + sin_part[:, :NZ])
    turned = along_z(jnp.concatenate(back, 1), tab_ref)
    return turned[:, :NZ], -turned[:, NZ:]


def stage_kernel(
    maps_in,
    kspace_in,
    mask_in,
    iterate_in,
    bits_in,
    adj_in,
    tab_in,
    k1_in,
    k2_in,
    k3_in,
    maps_ref,
    masked_ref,
    weight_ref,
    own_ref,
    edges_ref,
    tab_ref,
    first_ref,
    all_ref,
    mask_ref,
    bits_ref,
    k1_ref,
    k2_ref,
    k3_ref,
    sems,
):
    moves = (
        (k1_in, k1_ref),
        (k2_in, k2_ref),
        (k3_in, k3_ref),
        (iterate_in, own_ref.at[0:2]),
        (bits_in, bits_ref),
        (adj_in, own_ref.at[4:6]),
        (mask_in, mask_ref),
        (kspace_in, masked_ref),
        (maps_in, maps_ref),
        (tab_in, tab_ref),
    )
    copies = [pltpu.make_async_copy(s, d, sems.at[i]) for i, (s, d) in enumerate(moves)]
    for copy in copies:
        copy.start()
    for copy in copies[0:3]:
        copy.wait()
    build_tables(k1_ref, k2_ref, k3_ref, all_ref)
    for copy in copies[3:]:
        copy.wait()
    for ch in range(2):
        rows = own_ref[ch].astype(BF16)
        for dest in range(8):
            first_ref[dest, ch] = rows
    weight = mask_ref[...].astype(F32)
    weight_ref[...] = weight
    for ch in range(2):
        masked_ref[ch] = weight * masked_ref[ch]
        own_ref[2 + ch] = (2 * bits_ref[ch] - 1).astype(F32)
    edges = []
    for ch in (2, 3, 4, 5, 0, 1):
        rows = own_ref[ch]
        if ch < 2:
            rows = split(rows)[1].astype(F32)
        edges += [rows[0:4], rows[NYL - 4 : NYL]]
    edges_ref[...] = jnp.concatenate(edges, 0).astype(BF16)


def gradient_kernel(
    field_ref, maps_ref, masked_ref, weight_ref, edges_ref, tab_ref, out_ref, pad
):
    weight = weight_ref[...]
    map_re, map_im = maps_ref[0], maps_ref[1]
    re = field_ref[:, 0].astype(F32).reshape(NY, NZ)
    im = field_ref[:, 1].astype(F32).reshape(NY, NZ)
    f_re, f_im = forward(map_re * re - map_im * im, map_re * im + map_im * re, tab_ref)
    f_re = weight * f_re - masked_ref[0]
    f_im = weight * f_im - masked_ref[1]
    b_re, b_im = inverse(f_re, f_im, tab_ref)
    zero = jnp.zeros((4, NZ), F32)
    for ch in range(2):
        pad[ch, 0:4] = zero
        pad[ch, NY + 4 : NY + 8] = zero
    pad[0, 4 : NY + 4] = map_re * b_re + map_im * b_im
    pad[1, 4 : NY + 4] = map_re * b_im - map_im * b_re
    edges = edges_ref[...]
    for dest in range(8):
        for ch in range(2):
            out_ref[dest, HALO_ROWS * ch : HALO_ROWS * ch + HALO_ROWS] = pad[
                ch, NYL * dest : NYL * dest + HALO_ROWS
            ].astype(BF16)
        out_ref[dest, 80:128] = edges


def relax_kernel(got_ref, field_ref, own_ref, out_ref, relaxed_ref, pad, qpad, message):
    coil = lax.axis_index("coil")
    lower, upper = jnp.maximum(coil - 1, 0), jnp.minimum(coil + 1, 7)
    below = jnp.where(coil > 0, got_ref[lower, 80:128].astype(F32), 0.0)
    above = jnp.where(coil < 7, got_ref[upper, 80:128].astype(F32), 0.0)
    for ch in range(2):
        under = jnp.where(coil > 0, field_ref[lower, ch].astype(F32), 0.0)
        over = jnp.where(coil < 7, field_ref[upper, ch].astype(F32), 0.0)
        at = 32 + 8 * ch
        pad[ch, 0:4] = under[NYL - 4 : NYL] + below[at + 4 : at + 8]
        pad[ch, 4 : 4 + NYL] = own_ref[ch]
        pad[ch, 4 + NYL : HALO_ROWS] = over[0:4] + above[at : at + 4]
        rows = slice(HALO_ROWS * ch, HALO_ROWS * ch + HALO_ROWS)
        total = got_ref[0, rows].astype(F32)
        for source in range(1, 8):
            total = total + got_ref[source, rows].astype(F32)
        relaxed = pad[ch] - STEP * total
        relaxed_ref[ch] = relaxed[4 : 4 + NYL]
        for side in range(2):
            first = HALF * side
            message[side, PART_ROWS * ch : PART_ROWS * ch + PART_ROWS] = relaxed[
                first : first + PART_ROWS
            ]
    for ch in range(4):
        qpad[ch, 0:3] = below[ch * 8 + 5 : ch * 8 + 8]
        qpad[ch, 3 : 3 + NYL] = own_ref[2 + ch]
        qpad[ch, 3 + NYL : 7 + NYL] = above[ch * 8 : ch * 8 + 4]
        for side in range(2):
            first = HALF * side
            at = 2 * PART_ROWS + 22 * ch
            message[side, at : at + 22] = qpad[ch, first : first + 22]
    for side in range(2):
        rows = message[side].astype(BF16)
        for dest in range(8):
            out_ref[2 * dest + side] = rows


def dot_first(left, right):
    return lax.dot_general(left, right, (((0,), (0,)), ((), ())), preferred_element_type=F32)


def build_tables(k1_ref, k2_ref, k3_ref, all_ref):
    t2_ref, t2t_ref = all_ref.at[0:576, 0:768], all_ref.at[576:1152, 0:768]
    t1_ref, t3t_ref = all_ref.at[0:192, 768:1152], all_ref.at[192:384, 768:1152]
    t3_ref, t1t_ref = all_ref.at[1152:1200, 0:768], all_ref.at[1200:1248, 0:768]
    lane = lax.broadcasted_iota(jnp.int32, (24, 256), 1)
    row = lax.broadcasted_iota(jnp.int32, (24, 256), 0)
    tile24 = ((lane % 24 == row) & (lane < 240)).astype(BF16)
    window = jnp.where(lane < 240, lane // 24, 99)

    def tap(dx, dy, dz, flip):
        if flip:
            dx, dy, dz = 2 - dx, 2 - dy, 2 - dz
        return dx * 9 + dy * 3 + dz

    for target, flip in ((t2_ref, False), (t2t_ref, True)):
        for dz in range(3):
            for dx in range(3):
                spread = []
                for dy in range(3):
                    block = k2_ref[tap(dx, dy, dz, flip)]
                    spread.append(dot_first(block, tile24) if flip else mm(block, tile24))
                for yo in range(8):
                    value = jnp.zeros((24, 256), F32)
                    for dy in range(3):
                        value = jnp.where(window == yo + dy, spread[dy], value)
                    at = dz * 192 + yo * 24
                    target[at : at + 24, dx * 256 : dx * 256 + 256] = value.astype(BF16)

    lane = lax.broadcasted_iota(jnp.int32, (24, 384), 1)
    lane2 = lax.broadcasted_iota(jnp.int32, (2, 384), 1)
    row2 = lax.broadcasted_iota(jnp.int32, (2, 384), 0)
    tile2 = ((lane2 // 16) % 2 == row2).astype(BF16)
    group, offset = lane // 32, lane % 16
    for target, source, flip in ((t1_ref, k1_ref, False), (t3t_ref, k3_ref, True)):
        spread = []
        for dy in range(3):
            value = jnp.zeros((24, 384), F32)
            for dx in range(3):
                for dz in range(3):
                    block = dot_first(source[tap(dx, dy, dz, flip)], tile2)
                    value = jnp.where(group == dx * 3 + dz, block, value)
            spread.append(value)
        for yo in range(8):
            value = jnp.zeros((24, 384), F32)
            for dy in range(3):
                value = jnp.where(offset == yo + dy, spread[dy], value)
            target[yo * 24 : yo * 24 + 24, :] = value.astype(BF16)

    window8 = window[0:8] - lax.broadcasted_iota(jnp.int32, (8, 256), 0)
    for target, source, flip in ((t3_ref, k3_ref, False), (t1t_ref, k1_ref, True)):
        for dz in range(3):
            for dx in range(3):
                spread = [mm(source[tap(dx, dy, dz, flip)], tile24) for dy in range(3)]
                both = []
                for ch in range(2):
                    value = jnp.zeros((8, 256), F32)
                    for dy in range(3):
                        value = jnp.where(window8 == dy, spread[dy][ch : ch + 1], value)
                    both.append(value)
                target[dz * 16 : dz * 16 + 16, dx * 256 : dx * 256 + 256] = jnp.concatenate(
                    both, 0
                ).astype(BF16)


def join_z(parts, rows, half, at_low, at_high):
    lanes = slice(half * NZ, half * NZ + NZ)
    before = jnp.where(at_low, 0.0, pltpu.roll(parts[0:rows, lanes], 1, 1))
    after = jnp.where(at_high, 0.0, pltpu.roll(parts[2 * rows : 3 * rows, lanes], NZ - 1, 1))
    return parts[rows : 2 * rows, lanes] + (before + after)


def denoise_kernel(
    planes_ref,
    all_ref,
    send_ref,
    mine_ref,
    theirs_ref,
    pair_ref,
    image,
    cots,
    a1,
    s1,
    a2,
    e2,
    e1,
):
    t2_ref, t2t_ref = all_ref.at[0:576, 0:768], all_ref.at[576:1152, 0:768]
    t1_ref, t3t_ref = all_ref.at[0:192, 768:1152], all_ref.at[192:384, 768:1152]
    t3_ref, t1t_ref = all_ref.at[1152:1200, 0:768], all_ref.at[1200:1248, 0:768]
    coil, slab = lax.axis_index("coil"), lax.axis_index("slab")
    base, side = 2 * (slab // 2), slab % 2

    def inside(plane):
        return (plane >= 0) & (plane < 16)

    def at_edges(rows):
        column = lax.broadcasted_iota(jnp.int32, (rows, NZ), 1)
        return column == 0, column == NZ - 1

    low, high = at_edges(PART_ROWS)

    def stage(ref, j, ch, rows):
        count = rows.shape[0]
        ref[0, j, ch, 0:count] = jnp.where(low[:count], 0.0, pltpu.roll(rows, 1, 1))
        ref[1, j, ch, 0:count] = rows
        ref[2, j, ch, 0:count] = jnp.where(high[:count], 0.0, pltpu.roll(rows, NZ - 1, 1))
        for dz in range(3):
            ref[dz, j, ch, PART_ROWS:32] = jnp.zeros((8, NZ), F32)

    for j in range(10):
        plane = base - 4 + j
        keep = inside(plane)
        source = jnp.clip(plane, 0, 15)
        for ch in range(2):
            rows = planes_ref[source, PART_ROWS * ch : PART_ROWS * ch + PART_ROWS].astype(F32)
            stage(image, j, ch, jnp.where(keep, rows, 0.0))
        if 1 <= j < 9:
            for ch in range(4):
                at = 2 * PART_ROWS + 22 * ch
                rows = planes_ref[source, at : at + 22].astype(F32)
                for dz in range(3):
                    cots[dz, j - 1, ch, 16:24] = jnp.zeros((8, NZ), F32)
                stage(cots, j - 1, ch, jnp.where(keep, rows, 0.0))

    def usable(plane):
        return jnp.where(inside(plane), 1.0, 0.0)

    for j in range(8):
        a1[j, 576:640] = jnp.zeros((64, NZ), BF16)
        s1[j, 576:640] = jnp.zeros((64, NZ), F32)
    for j in range(6):
        e2[j, 480:640] = jnp.zeros((160, 2 * NZ), BF16)

    def rows_of(table_ref, rows):
        if rows == 192:
            return table_ref[...]
        return jnp.concatenate([table_ref[192 * dz : 192 * dz + rows] for dz in range(3)], 0)

    def first_step(step, carry):
        pair, block = 2 * (step // 3), step % 3
        at = pl.multiple_of(8 * block, 8)
        to = pl.multiple_of(192 * block, 192)
        pieces = []
        for dx in range(3):
            for dz in range(3):
                for ch in range(2):
                    pieces.append(
                        jnp.concatenate(
                            [
                                image[dz, pair + dx, ch, pl.ds(at, 16)],
                                image[dz, pair + dx + 1, ch, pl.ds(at, 16)],
                            ],
                            1,
                        ).astype(BF16)
                    )
        both = mm(t1_ref[:, 0:288], jnp.concatenate(pieces, 0))
        for half in range(2):
            pre = both[:, half * NZ : half * NZ + NZ]
            gate = jax.nn.sigmoid(pre)
            keep = usable(base - 3 + pair + half)
            a1[pair + half, pl.ds(to, 192)] = (pre * gate * keep).astype(BF16)
            s1[pair + half, pl.ds(to, 192)] = gate * (1.0 + pre * (1.0 - gate)) * keep
        return carry

    lax.fori_loop(0, 12, first_step, 0, unroll=12)

    def clear(ref, planes, top, bottom):
        rows = ref.shape[1]
        first, last = (coil == 0) & (side == 0), (coil == 7) & (side == 1)
        for j in range(planes):
            value = ref[j, 0:top]
            ref[j, 0:top] = jnp.where(first, jnp.zeros_like(value), value)
            value = ref[j, bottom:rows]
            ref[j, bottom:rows] = jnp.where(last, jnp.zeros_like(value), value)

    clear(a1, 8, 72, 456)

    def second_block(pair, at, to, rows):
        stacked = jnp.concatenate(
            [
                jnp.concatenate(
                    [a1[pair + dx, pl.ds(to, 256)], a1[pair + dx + 1, pl.ds(to, 256)]], 1
                )
                for dx in range(3)
            ],
            0,
        )
        parts = mm(rows_of(t2_ref, rows), stacked)
        low, high = at_edges(rows)
        for half in range(2):
            pre = join_z(parts, rows, half, low, high)
            gate = jax.nn.sigmoid(pre)
            keep = usable(base - 2 + pair + half)
            a2[pair + half, pl.ds(to, rows)] = (pre * gate * keep).astype(BF16)
            slope = gate * (1.0 + pre * (1.0 - gate)) * keep
            pieces = []
            for dx in range(3):
                for dz in range(3):
                    for ch in range(2):
                        pieces.append(
                            jnp.concatenate(
                                [
                                    cots[dz, pair + half + dx, ch, pl.ds(at, 16)],
                                    cots[dz, pair + half + dx, 2 + ch, pl.ds(at, 16)],
                                ],
                                1,
                            ).astype(BF16)
                        )
            back = mm(t3t_ref[0:rows, 0:288], jnp.concatenate(pieces, 0))
            for which in range(2):
                lanes = slice(which * NZ, which * NZ + NZ)
                e2[pair + half, pl.ds(to, rows), lanes] = (back[:, lanes] * slope).astype(BF16)

    def second_step(step, carry):
        pair = 2 * step
        second_block(pair, 0, 0, 192)
        second_block(pair, 8, 192, 192)
        second_block(pair, 16, 384, 96)
        return carry

    lax.fori_loop(0, 3, second_step, 0, unroll=3)
    clear(a2, 6, 48, 432)
    clear(e2, 6, 48, 432)

    def third_block(plane, to, rows):
        stacked = jnp.concatenate([e2[plane + dx, pl.ds(to, 256)] for dx in range(3)], 0)
        back = mm(rows_of(t2t_ref, rows), stacked)
        low, high = at_edges(rows)
        slope = s1[plane + 2, pl.ds(to + 48, rows)]
        for which in range(2):
            grad = join_z(back, rows, which, low, high) * slope
            e1[plane, pl.ds(to, rows), which * NZ : which * NZ + NZ] = grad.astype(BF16)

    def third_step(step, carry):
        for plane in (2 * step, 2 * step + 1):
            third_block(plane, 0, 192)
            third_block(plane, 192, 192)
            third_block(plane, 384, 48)
        return carry

    lax.fori_loop(0, 2, third_step, 0, unroll=2)
    for j in range(4):
        e1[j, 432:448] = jnp.zeros((16, 2 * NZ), BF16)
    clear(e1, 4, 24, 408)

    low, high = at_edges(16)
    for block in range(2):
        rows = slice(8 * block, 8 * block + 8)
        window = slice(24 + 192 * block, 280 + 192 * block)
        stacked = jnp.concatenate(
            [jnp.concatenate([a2[1 + dx, window], a2[2 + dx, window]], 1) for dx in range(3)], 0
        )
        parts = mm(t3_ref[...], stacked)
        for p in range(2):
            update = join_z(parts, 16, p, low, high)
            for ch in range(2):
                pair_ref[p, 4 + ch, rows] = update[8 * ch : 8 * ch + 8]

    for p in range(2):
        for block in range(2):
            rows = slice(8 * block, 8 * block + 8)
            shifted = slice(3 + 8 * block, 11 + 8 * block)
            window = slice(192 * block, 192 * block + 256)
            stacked = jnp.concatenate([e1[p + dx, window] for dx in range(3)], 0)
            back = mm(t1t_ref[...], stacked)
            for which in range(2):
                grad = join_z(back, 16, which, low, high)
                for ch in range(2):
                    pair_ref[p, 2 * which + ch, rows] = grad[8 * ch : 8 * ch + 8]
        for ch in range(4):
            pulled = cots[1, 3 + p, ch, 3 : 3 + HALF] + pair_ref[p, ch]
            pulled = pulled.astype(BF16)
            for dest in range(8):
                send_ref[2 * dest + p, ch] = pulled
    mine_ref[...] = pair_ref[side]
    theirs_ref[...] = pair_ref[1 - side]


def normal_kernel(field_ref, maps_ref, weight_ref, tab_ref, out_ref):
    weight = weight_ref[...]
    map_re, map_im = maps_ref[0], maps_ref[1]

    def over_z(rows):
        rows = rows.astype(BF16)
        return mm(rows, tab_ref[1024:1280]) + mm(rows, tab_ref[1280:1536])

    def over_y(columns):
        columns = columns.astype(BF16)
        return mm(tab_ref[0:512], columns) + mm(tab_ref[512:1024], columns)

    rows = []
    for which in range(2):
        re = field_ref[:, 2 * which].reshape(NY, NZ).astype(F32)
        im = field_ref[:, 2 * which + 1].reshape(NY, NZ).astype(F32)
        rows.append(
            jnp.concatenate([map_re * re - map_im * im, map_re * im + map_im * re], 1)
        )
    turned = over_z(jnp.concatenate(rows, 0))
    turned = over_y(jnp.concatenate([turned[:NY], turned[NY:]], 1))
    columns = []
    for which in range(2):
        at = 2 * NZ * which
        cos_part, sin_part = turned[:NY, at : at + 2 * NZ], turned[NY:, at : at + 2 * NZ]
        columns.append(weight * (cos_part[:, :NZ] + sin_part[:, NZ:]))
        columns.append(weight * (cos_part[:, NZ:] - sin_part[:, :NZ]))
    turned = over_y(jnp.concatenate(columns, 1))
    rows = []
    for which in range(2):
        at = 2 * NZ * which
        cos_part, sin_part = turned[:NY, at : at + 2 * NZ], turned[NY:, at : at + 2 * NZ]
        rows.append(
            jnp.concatenate(
                [cos_part[:, :NZ] - sin_part[:, NZ:], -(cos_part[:, NZ:] + sin_part[:, :NZ])], 1
            )
        )
    turned = over_z(jnp.concatenate(rows, 0))
    for which in range(2):
        back = turned[NY * which : NY * which + NY]
        b_re, b_im = back[:, :NZ], -back[:, NZ:]
        out_re = (map_re * b_re + map_im * b_im).astype(BF16)
        out_im = (map_re * b_im - map_im * b_re).astype(BF16)
        for dest in range(8):
            rows = slice(NYL * dest, NYL * dest + NYL)
            out_ref[dest, 2 * which] = out_re[rows]
            out_ref[dest, 2 * which + 1] = out_im[rows]


def final_kernel(
    got_ref, mine_ref, theirs_ref, relaxed_ref, own_ref, loss_ref, new_ref, probe_ref, next_ref
):
    side = lax.axis_index("slab") % 2
    sums = []
    for ch in range(4):
        total = got_ref[0, ch].astype(F32)
        for source in range(1, 8):
            total = total + got_ref[source, ch].astype(F32)
        sums.append(STEP * total)

    def put(first, part_ref):
        rows = slice(first, first + HALF)
        for ch in range(2):
            new_ref[ch, rows] = relaxed_ref[ch, rows] + part_ref[4 + ch]
            probe_ref[ch, rows] = own_ref[2 + ch, rows] + part_ref[ch] - sums[ch][rows]
            pulled = own_ref[4 + ch, rows] + part_ref[2 + ch]
            next_ref[ch, rows] = loss_ref[ch, rows] + (pulled - sums[2 + ch][rows])

    @pl.when(side == 0)
    def _():
        put(0, mine_ref)
        put(HALF, theirs_ref)

    @pl.when(side == 1)
    def _():
        put(0, theirs_ref)
        put(HALF, mine_ref)


def on_device(
    coil_maps,
    kspace,
    sample_mask,
    iterate,
    probe_bits,
    loss_gradient,
    adjoint,
    kernel_first,
    kernel_second,
    kernel_last,
):
    maps = coil_maps[0, :, 0]
    data = kspace[0, :, 0]
    iterate, bits, loss, adj = (a[:, 0] for a in (iterate, probe_bits, loss_gradient, adjoint))
    slabs = lax.axis_size("slab")
    coils = lax.axis_size("coil")
    families = [
        [c * slabs + 2 * j + h for c in range(coils) for h in range(2)] for j in range(slabs // 2)
    ]

    k1 = jnp.transpose(kernel_first, (2, 3, 4, 1, 0)).reshape(27, 2, 24)
    k2 = jnp.transpose(kernel_second, (2, 3, 4, 0, 1)).reshape(27, 24, 24)
    k3 = jnp.transpose(kernel_last, (2, 3, 4, 0, 1)).reshape(27, 2, 24)
    staged = pl.pallas_call(
        stage_kernel,
        compiler_params=GRANT,
        out_shape=[
            jax.ShapeDtypeStruct((2, NY, NZ), F32),
            jax.ShapeDtypeStruct((2, NY, NZ), F32),
            jax.ShapeDtypeStruct((NY, NZ), F32),
            jax.ShapeDtypeStruct((6, NYL, NZ), F32),
            jax.ShapeDtypeStruct((48, NZ), BF16),
            jax.ShapeDtypeStruct((1536, 256), BF16),
            jax.ShapeDtypeStruct((8, 2, NYL, NZ), BF16),
            jax.ShapeDtypeStruct((1248, 1152), BF16),
        ],
        in_specs=[pl.BlockSpec(memory_space=pltpu.HBM)] * 10,
        out_specs=whole(8),
        scratch_shapes=[
            pltpu.VMEM((NY, NZ), jnp.int32),
            pltpu.VMEM((2, NYL, NZ), jnp.int32),
            pltpu.VMEM((27, 2, 24), BF16),
            pltpu.VMEM((27, 24, 24), BF16),
            pltpu.VMEM((27, 2, 24), BF16),
            pltpu.SemaphoreType.DMA((10,)),
        ],
    )(
        *(
            pltpu.with_memory_space_constraint(x, pltpu.HBM)
            for x in (
                maps, data, sample_mask, iterate, bits, adj, fourier_constants(), k1, k2, k3
            )
        )
    )
    maps, masked, weight, own, edges, fourier, first, toeplitz = staged
    field = lax.all_to_all(first, "coil", 0, 0)
    partial_sums = pl.pallas_call(
        gradient_kernel,
        compiler_params=GRANT,
        out_shape=jax.ShapeDtypeStruct((8, 128, NZ), BF16),
        in_specs=whole(6),
        out_specs=whole(1)[0],
        scratch_shapes=[pltpu.VMEM((2, NY + 8, NZ), F32)],
    )(field, maps, masked, weight, edges, fourier)
    got = lax.all_to_all(partial_sums, "coil", 0, 0)
    payload, relaxed = pl.pallas_call(
        relax_kernel,
        compiler_params=GRANT,
        out_shape=[
            jax.ShapeDtypeStruct((16, MESSAGE, NZ), BF16),
            jax.ShapeDtypeStruct((2, NYL, NZ), F32),
        ],
        in_specs=whole(3),
        out_specs=whole(2),
        scratch_shapes=[
            pltpu.VMEM((2, HALO_ROWS, NZ), F32),
            pltpu.VMEM((4, HALO_ROWS, NZ), F32),
            pltpu.VMEM((2, MESSAGE, NZ), F32),
        ],
    )(got, field, own)
    planes = lax.all_to_all(payload, "slab", 0, 0)
    send, mine, theirs = pl.pallas_call(
        denoise_kernel,
        compiler_params=GRANT,
        out_shape=[
            jax.ShapeDtypeStruct((16, 4, HALF, NZ), BF16),
            jax.ShapeDtypeStruct((6, HALF, NZ), F32),
            jax.ShapeDtypeStruct((6, HALF, NZ), F32),
        ],
        in_specs=whole(2),
        out_specs=whole(3),
        scratch_shapes=[
            pltpu.VMEM((2, 6, HALF, NZ), F32),
            pltpu.VMEM((3, 10, 2, 32, NZ), F32),
            pltpu.VMEM((3, 8, 4, 32, NZ), F32),
            pltpu.VMEM((8, 640, NZ), BF16),
            pltpu.VMEM((8, 640, NZ), F32),
            pltpu.VMEM((6, 480, NZ), BF16),
            pltpu.VMEM((6, 640, 2 * NZ), BF16),
            pltpu.VMEM((4, 448, 2 * NZ), BF16),
        ],
    )(planes, toeplitz)
    spread = lax.all_to_all(send, ("coil", "slab"), 0, 0, axis_index_groups=families)
    theirs = lax.ppermute(theirs, "slab", [(i, i + 1 - 2 * (i % 2)) for i in range(slabs)])
    back = pl.pallas_call(
        normal_kernel,
        compiler_params=GRANT,
        out_shape=jax.ShapeDtypeStruct((8, 4, NYL, NZ), BF16),
        in_specs=whole(4),
        out_specs=whole(1)[0],
    )(spread, maps, weight, fourier)
    back = lax.all_to_all(back, "coil", 0, 0)
    new_iterate, probe, following = pl.pallas_call(
        final_kernel,
        compiler_params=GRANT,
        out_shape=[jax.ShapeDtypeStruct((2, NYL, NZ), F32)] * 3,
        in_specs=whole(6),
        out_specs=whole(3),
    )(back, mine, theirs, relaxed, own, loss)
    return new_iterate[:, None], probe[:, None], following[:, None]


def solution(mesh):
    image = P(None, "slab", "coil", None)
    coils = P("coil", None, "slab", None, None)
    return jax.shard_map(
        on_device,
        mesh=mesh,
        in_specs=(coils, coils, P(), image, image, image, image, P(), P(), P()),
        out_specs=(image, image, image),
        check_vma=False,
    )
```
